256 devices in a mesh: rows: 32 (over x, y, core), hst: 8 (over z).
Axes of the slice: x: 4, y: 4, z: 8, core: 2. Of those that a mesh axis runs over, the one named last changes fastest.
Arguments:
- grad_pooled: bfloat16 [16384, 4, 128], P(('rows', 'hst')), may hold values from -6 to 6
- weights: bfloat16 [16384, 4, 40], P(('rows', 'hst')), may hold values from 0.25 to 1.75
- owner: int32 [16384, 4, 40], P(('rows', 'hst')), may hold values from 0 to 255, as said below
- slot: int32 [16384, 4, 40], P(('rows', 'hst')), may hold values from 0 to 2047, as said below
- lengths: int32 [16384, 4], P(('rows', 'hst')), may hold values from 10 to 40
- counts: int32 [256], P(('rows', 'hst')), may hold values from 1024 to 2048, as said below
- table: float32 [524288, 128], P(('rows', 'hst')), may hold values from -0.6 to 0.6
- states: float32 [524288], P(('rows', 'hst')), may hold values from 0.5 to 20
Outputs:
- weight_grad: float32 [16384, 4, 40], P(('rows', 'hst'))
- new_table: float32 [524288, 128], P(('rows', 'hst'))
- new_states: float32 [524288], P(('rows', 'hst'))
The draws below stay inside these ranges and needn't reach their ends.
Inputs may be any that keep to these rules, and one draw needn't show every extreme that they name: Among the ids of one device's samples, no owner appears more than 96 times, and in every draw some owner appears exactly 96 times among the ids of every device. Each id's slot is below the count of its owner. `counts`: some device's count is 2048.
All inputs are finite; a program needn't handle non-finite values.
Results may differ from the reference program's by a relative error of at most 0.0003.
Values may be sent and summed in bfloat16 or wider, within the bound.
A program may use at most 128 MiB of HBM per device.

```python
import math
import jax
import jax.numpy as jnp
from jax import lax

D = 128
F = 4
L = 40
B_DEV = 64
TOUCH = 2048
CAP = 96
SAMPLES = 16384
ROWS_ALL = 524288
DEVICES = 256


def routing(key):
    ids_dev = B_DEV * F * L
    hottest = max(1, ids_dev // (4 * CAP))
    first, second, third, fourth = jax.random.split(jax.random.fold_in(key, 7), 4)
    ranking = jax.random.permutation(first, DEVICES)
    position = jnp.arange(ids_dev, dtype=jnp.int32)
    rank = jnp.where(position < hottest * CAP, position // CAP, hottest + (position - hottest * CAP) % (DEVICES - hottest))
    base = ranking[rank]
    keys = jax.random.split(second, DEVICES)
    shuffles = jax.vmap(lambda single: jax.random.permutation(single, ids_dev))(keys)
    owner = base[shuffles].reshape(SAMPLES, F, L).astype(jnp.int32)
    counts = jax.random.randint(third, (DEVICES,), TOUCH // 2, TOUCH + 1).astype(jnp.int32)
    counts = counts.at[ranking[0]].set(TOUCH)
    raw = jax.random.randint(fourth, (SAMPLES, F, L), 0, 1 << 20).astype(jnp.int32)
    slot = raw % counts[owner]
    return (owner, slot.astype(jnp.int32), counts)


def draw_owner(key, part):
    return routing(key)[0]


def draw_slot(key, part):
    return routing(key)[1]


def draw_counts(key, part):
    return routing(key)[2]


def touch_ends(entries, stream_key, low, top_value):
    extent = entries.shape
    spot = [jax.random.randint(jax.random.fold_in(stream_key, axis), (), 0, extent[axis]) for axis in range(len(extent))]
    entries = entries.at[tuple(spot)].set(low)
    longest = extent.index(max(extent))
    spot[longest] = (spot[longest] + 1) % extent[longest]
    return entries.at[tuple(spot)].set(top_value)


def shard_levels(own_key, extent, cuts, least, largest):
    def one(dim, shards_of):
        draws = jax.random.uniform(jax.random.fold_in(jax.random.fold_in(own_key, 6), dim), (shards_of,), jnp.float32, least / len(cuts), largest / len(cuts))
        return jnp.repeat(jnp.exp(draws), extent[dim] // shards_of).reshape((-1,) + (1,) * (len(extent) - dim - 1))

    factor_of = one(*cuts[0])
    for cut in cuts[1:]:
        factor_of = factor_of * one(*cut)
    return factor_of


def gaussian(key, extent, scale, reach, shards=(), held_as=jnp.bfloat16):
    result = scale * jax.random.normal(key, extent, jnp.float32)
    if shards:
        result = result * shard_levels(key, extent, shards, -0.22, 0.18)
    return jnp.clip(result, -reach, reach).astype(held_as)


def setup_inputs(seed: int = 0) -> dict:
    key_list = jax.random.split(jax.random.key(seed), 9)
    return {
        "grad_pooled": gaussian(key_list[0], (SAMPLES, F, D), 1.0, 6.0, ((0, 256),)),
        "weights": jnp.clip(0.25 + 1.5 * jax.random.uniform(key_list[1], (SAMPLES, F, L), jnp.float32) ** shard_levels(key_list[1], (SAMPLES, F, L), ((0, 256),), -0.2, 0.2), 0.25, 1.75).astype(jnp.bfloat16),
        "owner": draw_owner(jax.random.fold_in(key_list[8], 71), 0),
        "slot": draw_slot(jax.random.fold_in(key_list[8], 71), 0),
        "lengths": touch_ends(jax.random.randint(key_list[4], (SAMPLES, F), L // 4, L + 1), jax.random.fold_in(key_list[4], 1), L // 4, L).astype(jnp.int32),
        "counts": draw_counts(jax.random.fold_in(key_list[8], 71), 0),
        "table": gaussian(key_list[6], (ROWS_ALL, D), 0.1, 0.6, ((0, 256),), jnp.float32),
        "states": jnp.clip(jnp.exp(math.log(20.0) - 3.6888795 * jax.random.uniform(key_list[7], (ROWS_ALL,), jnp.float32) ** shard_levels(key_list[7], (ROWS_ALL,), ((0, 256),), -0.2, 0.2)), 0.5, 20.0),
    }


learn_rate = 0.1
epsilon_value = 1e-08

def reference(grad_pooled, weights, owner, slot, lengths, counts, table, states):
    samples = weights.shape[0]
    block = math.gcd(samples, 256)
    width = table.shape[1]
    live = jnp.arange(L, dtype=jnp.int32)[None, None, :] < lengths[:, :, None]
    scaled = jnp.where(live, weights.astype(jnp.float32), jnp.zeros(weights.shape, jnp.float32))
    flat = (owner * TOUCH + slot).astype(jnp.int32)

    def visit(index, carry):
        grad_sum, products = carry
        start = index * block
        pooled = lax.dynamic_slice_in_dim(grad_pooled, start, block, 0).astype(jnp.float32)
        places = lax.dynamic_slice_in_dim(flat, start, block, 0)
        factor = lax.dynamic_slice_in_dim(scaled, start, block, 0)
        alive = lax.dynamic_slice_in_dim(live, start, block, 0)
        rows_at = table[places]
        dots = lax.optimization_barrier(jnp.sum(pooled[:, :, None, :] * rows_at, axis=-1))
        dots = jnp.where(alive, dots, jnp.zeros(dots.shape, dots.dtype))
        products = lax.dynamic_update_slice_in_dim(products, dots, start, 0)
        terms = factor[..., None] * pooled[:, :, None, :]
        grad_sum = grad_sum.at[places.reshape(-1)].add(terms.reshape(-1, width))
        return (grad_sum, products)
    start_sum = jnp.zeros(table.shape, jnp.float32)
    start_products = jnp.zeros(weights.shape, jnp.float32)
    row_grad, weight_grad = lax.fori_loop(0, samples // block, visit, (start_sum, start_products))
    summed = states + lax.optimization_barrier(jnp.mean(row_grad * row_grad, axis=-1))
    updated = table - learn_rate * row_grad / (jnp.sqrt(summed)[:, None] + epsilon_value)
    keep = (jnp.arange(TOUCH, dtype=jnp.int32)[None, :] < counts[:, None]).reshape(-1)
    new_table = jnp.where(keep[:, None], updated, jnp.zeros(updated.shape, updated.dtype))
    new_states = jnp.where(keep, summed, jnp.zeros(summed.shape, summed.dtype))
    return (weight_grad, new_table, new_states)
```

```python
import functools
import jax
import jax.numpy as jnp
import numpy as np
from jax import lax
from jax.experimental import pallas as pl
from jax.experimental.pallas import tpu as pltpu
from jax.sharding import PartitionSpec as P

learn_rate = 0.1
epsilon_value = 1e-08
CAP = 96
RP = 128
BOTH = ("rows", "hst")
BF = jnp.bfloat16
F32 = jnp.float32
I32 = jnp.int32


def onehot(mask):
    return jnp.where(mask, 1.0, 0.0).astype(BF)


def iota(shape, dim):
    return lax.broadcasted_iota(I32, shape, dim)


def params(*sem):
    return pltpu.CompilerParams(dimension_semantics=sem or None)


def route_kernel(own_ref, slot_ref, bag_ref, w_ref, meta_ref, bags_ref, rank_ref, acc, base, upper):
    steps, k = own_ref.shape
    n = acc.shape[0]
    acc[...] = jnp.zeros_like(acc)
    base[...] = jnp.zeros_like(base)
    upper[...] = onehot(iota((k, k), 0) < iota((k, k), 1))

    def step(i, carry):
        row = pl.ds(i, 1)
        mask = iota((n, k), 0) == own_ref[row, :]
        a = onehot(mask)
        before = jnp.dot(a, upper[...], preferred_element_type=F32)
        start = jnp.concatenate([base[...]] * (k // RP), axis=1)
        rank = jnp.sum(jnp.where(mask, before + start, 0.0), axis=0, keepdims=True)
        base[...] += jnp.dot(a, jnp.ones((k, RP), BF), preferred_element_type=F32)
        rank = rank.astype(I32)
        rank_ref[row, :] = rank
        put = iota((RP, k), 0) == rank
        slot = slot_ref[row, :]
        parts = [
            (slot >> 8).astype(F32),
            (slot & 255).astype(F32),
            bag_ref[row, :].astype(F32),
            w_ref[row, :],
        ]
        b = jnp.concatenate([jnp.where(put, p, 0.0).astype(BF) for p in parts], axis=0)
        acc[...] += lax.dot_general(a, b, (((1,), (1,)), ((), ())), preferred_element_type=F32)
        return carry

    lax.fori_loop(0, steps, step, 0)
    meta_ref[:, 0:RP] = acc[:, 0:RP] * 256.0 + acc[:, RP : 2 * RP]
    bags_ref[...] = acc[:, 2 * RP : 3 * RP].astype(I32)
    meta_ref[:, RP : 2 * RP] = acc[:, 3 * RP : 4 * RP]


def send_kernel(bag_ref, g_ref, out_ref):
    owners = bag_ref.shape[0]
    bags = g_ref.shape[0]
    pieces = [onehot(iota((bags, RP), 0) == bag_ref[i : i + 1, :]) for i in range(owners)]
    pick = jnp.concatenate(pieces, axis=1)
    rows = lax.dot_general(pick, g_ref[...], (((0,), (0,)), ((), ())), preferred_element_type=F32)
    rows = rows.astype(BF)
    for i in range(owners):
        out_ref[i] = rows[i * RP : i * RP + CAP]


def spots(slot, k):
    hi = jnp.broadcast_to((slot >> 4).astype(F32), (16, k)).astype(BF)
    lo = jnp.broadcast_to((slot & 15).astype(F32), (16, k)).astype(BF)
    return hi, lo == iota((16, k), 0).astype(F32).astype(BF)


def tile_of(hi, base, first, count):
    zero = jnp.zeros_like(base)
    return jnp.concatenate(
        [jnp.where(hi == jnp.asarray(first + t, BF), base, zero) for t in range(count)], axis=0
    )


def rows_kernel(live_ref, slot_ref, table_ref, out_ref, tab):
    c = pl.program_id(0)
    touched, width = table_ref.shape
    k = slot_ref.shape[1]

    @pl.when(c == 0)
    def _():
        for m in range(touched // 128):
            t = table_ref[m * 128 : (m + 1) * 128, :].T
            high = t.astype(BF)
            tab[0:width, m * 128 : (m + 1) * 128] = high
            tab[width : 2 * width, m * 128 : (m + 1) * 128] = (t - high.astype(F32)).astype(BF)

    @pl.when(live_ref[c] != 0)
    def _():
        hi, at = spots(slot_ref[pl.ds(c, 1), :], k)
        base = jnp.where(at, jnp.ones((16, k), BF), jnp.zeros((16, k), BF))
        total = jnp.zeros((2 * width, k), F32)
        for m in range(touched // 256):
            s = tile_of(hi, base, 16 * m, 16)
            total += jnp.dot(tab[:, m * 256 : (m + 1) * 256], s, preferred_element_type=F32)
        out_ref[...] = total[0:width] + total[width:]


def owner_kernel(
    live_ref, count_ref, slot_ref, w_ref, rows_ref, g_ref, table_ref, states_ref,
    prod_ref, new_table_ref, new_states_ref, grad,
):
    c = pl.program_id(0)
    touched, width = table_ref.shape
    k = slot_ref.shape[1]

    @pl.when(c == 0)
    def _():
        grad[...] = jnp.zeros_like(grad)
        prod_ref[...] = jnp.zeros_like(prod_ref)

    @pl.when(live_ref[c] != 0)
    def _():
        g = g_ref[...].reshape(k, width)
        row = pl.ds(c, 1)
        hi, at = spots(slot_ref[row, :], k)
        w = jnp.broadcast_to(w_ref[row, :], (16, k)).astype(BF)
        base = jnp.where(at, w, jnp.zeros_like(w))
        for m in range(touched // 256):
            s = tile_of(hi, base, 16 * m, 16)
            grad[m * 256 : (m + 1) * 256, :] += jnp.dot(s, g, preferred_element_type=F32)
        prod_ref[row, :] = jnp.sum(rows_ref[...] * g.astype(F32).T, axis=0, keepdims=True)

    @pl.when(c == pl.num_programs(0) - 1)
    def _():
        eye = iota((128, 128), 0) == iota((128, 128), 1)
        for m in range(touched // 128):
            rows = slice(m * 128, (m + 1) * 128)
            r = grad[rows, :]
            state = jnp.sum(jnp.where(eye, states_ref[m : m + 1, :], 0.0), axis=1, keepdims=True)
            summed = state + jnp.mean(r * r, axis=1, keepdims=True)
            updated = table_ref[rows, :] - learn_rate * r / (jnp.sqrt(summed) + epsilon_value)
            keep = iota((128, 128), 0) + m * 128 < count_ref[0]
            new_table_ref[rows, :] = jnp.where(keep, updated, 0.0)
            new_states_ref[m : m + 1, :] = jnp.sum(
                jnp.where(eye & keep, summed, 0.0), axis=0, keepdims=True
            )


def back_kernel(own_ref, rank_ref, prod_ref, out_ref, parts):
    steps, k = own_ref.shape
    n = prod_ref.shape[0]
    t = prod_ref[...].T
    high = t.astype(BF)
    rest = t - high.astype(F32)
    mid = rest.astype(BF)
    parts[0:RP, :] = high
    parts[RP : 2 * RP, :] = mid
    parts[2 * RP : 3 * RP, :] = (rest - mid.astype(F32)).astype(BF)

    def step(i, carry):
        row = pl.ds(i, 1)
        a = onehot(iota((n, k), 0) == own_ref[row, :])
        x = jnp.dot(parts[...], a, preferred_element_type=F32)
        x = (x[2 * RP :] + x[RP : 2 * RP]) + x[0:RP]
        out_ref[row, :] = jnp.sum(
            jnp.where(iota((RP, k), 0) == rank_ref[row, :], x, 0.0), axis=0, keepdims=True
        )
        return carry

    lax.fori_loop(0, steps, step, 0)


def local(grad_pooled, weights, owner, slot, lengths, counts, table, states):
    devices = lax.axis_size("rows") * lax.axis_size("hst")
    bags, features, per_bag = weights.shape
    width = grad_pooled.shape[2]
    touched = table.shape[0]
    total_ids = bags * features * per_bag
    n_bags = bags * features
    k1 = 256
    steps = total_ids // k1
    vmem = pl.BlockSpec(memory_space=pltpu.VMEM)
    live = jnp.arange(per_bag, dtype=I32)[None, None, :] < lengths[:, :, None]
    own = jnp.where(live, owner, -1).reshape(steps, k1)
    slots = slot.reshape(steps, k1)
    w = weights.astype(F32).reshape(steps, k1)
    bag = jnp.asarray((np.arange(total_ids) // per_bag).reshape(steps, k1), I32)
    g = grad_pooled.reshape(n_bags, width)

    meta, send_bags, rank = pl.pallas_call(
        route_kernel,
        out_shape=(
            jax.ShapeDtypeStruct((devices, 2 * RP), F32),
            jax.ShapeDtypeStruct((devices, RP), I32),
            jax.ShapeDtypeStruct((steps, k1), I32),
        ),
        in_specs=[vmem] * 4,
        out_specs=(vmem,) * 3,
        scratch_shapes=[
            pltpu.VMEM((devices, 4 * RP), F32),
            pltpu.VMEM((devices, RP), F32),
            pltpu.VMEM((k1, k1), BF),
        ],
        name="route",
    )(own, slots, bag, w)
    got_meta = lax.all_to_all(meta, BOTH, split_axis=0, concat_axis=0, tiled=True)

    group = 16
    send = pl.pallas_call(
        send_kernel,
        grid=(devices // group,),
        out_shape=jax.ShapeDtypeStruct((devices, CAP, width), BF),
        in_specs=[
            pl.BlockSpec((group, RP), lambda i: (i, 0)),
            pl.BlockSpec((n_bags, width), lambda i: (0, 0)),
        ],
        out_specs=pl.BlockSpec((group, CAP, width), lambda i: (i, 0, 0)),
        name="send",
    )(send_bags, g)
    got = lax.all_to_all(send, BOTH, split_axis=0, concat_axis=0, tiled=True)

    srcs = 32
    tiles = CAP // 16
    chunks = devices // srcs * tiles
    k2 = srcs * 16

    def by_chunk(v):
        v = v[:, :CAP].reshape(devices // srcs, srcs, tiles, 16)
        return v.transpose(0, 2, 1, 3).reshape(chunks, k2)

    got_slot = by_chunk(got_meta[:, :RP].astype(I32))
    got_w = by_chunk(got_meta[:, RP:])
    active = (jnp.max(got_w, axis=1) > 0.0).astype(I32)
    ids = chunks * k2

    rows_t = pl.pallas_call(
        rows_kernel,
        grid_spec=pltpu.PrefetchScalarGridSpec(
            num_scalar_prefetch=1,
            grid=(chunks,),
            in_specs=[
                pl.BlockSpec((chunks, k2), lambda c, *_: (0, 0)),
                pl.BlockSpec((touched, width), lambda c, *_: (0, 0)),
            ],
            out_specs=pl.BlockSpec((width, k2), lambda c, *_: (0, c)),
            scratch_shapes=[pltpu.VMEM((2 * width, touched), BF)],
        ),
        out_shape=jax.ShapeDtypeStruct((width, ids), F32),
        cost_estimate=pl.CostEstimate(
            flops=4 * ids * touched * width, bytes_accessed=ids * width * 4, transcendentals=0
        ),
        compiler_params=params("arbitrary"),
        name="table_rows",
    )(active, got_slot, table)

    prods, new_table, new_states = pl.pallas_call(
        owner_kernel,
        grid_spec=pltpu.PrefetchScalarGridSpec(
            num_scalar_prefetch=2,
            grid=(chunks,),
            in_specs=[
                pl.BlockSpec((chunks, k2), lambda c, *_: (0, 0)),
                pl.BlockSpec((chunks, k2), lambda c, *_: (0, 0)),
                pl.BlockSpec((width, k2), lambda c, *_: (0, c)),
                pl.BlockSpec((srcs, 16, width), lambda c, *_: (c // tiles, c % tiles, 0)),
                pl.BlockSpec((touched, width), lambda c, *_: (0, 0)),
                pl.BlockSpec((touched // 128, 128), lambda c, *_: (0, 0)),
            ],
            out_specs=(
                pl.BlockSpec((chunks, k2), lambda c, *_: (0, 0)),
                pl.BlockSpec((touched, width), lambda c, *_: (0, 0)),
                pl.BlockSpec((touched // 128, 128), lambda c, *_: (0, 0)),
            ),
            scratch_shapes=[pltpu.VMEM((touched, width), F32)],
        ),
        out_shape=(
            jax.ShapeDtypeStruct((chunks, k2), F32),
            jax.ShapeDtypeStruct((touched, width), F32),
            jax.ShapeDtypeStruct((touched // 128, 128), F32),
        ),
        compiler_params=params("arbitrary"),
        name="owner_step",
    )(active, counts, got_slot, got_w, rows_t, got, table, states.reshape(touched // 128, 128))

    back = prods.reshape(devices // srcs, tiles, srcs, 16).transpose(0, 2, 1, 3).reshape(devices, CAP)
    back = jnp.pad(back, ((0, 0), (0, RP - CAP)))
    returned = lax.all_to_all(back, BOTH, split_axis=0, concat_axis=0, tiled=True)
    weight_grad = pl.pallas_call(
        back_kernel,
        out_shape=jax.ShapeDtypeStruct((steps, k1), F32),
        in_specs=[vmem] * 3,
        out_specs=vmem,
        scratch_shapes=[pltpu.VMEM((3 * RP, devices), BF)],
        name="back",
    )(own, rank, returned)
    return (weight_grad.reshape(weights.shape), new_table, new_states.reshape(-1))


def solution(mesh):
    return jax.shard_map(
        local,
        mesh=mesh,
        in_specs=(
            P(BOTH, None, None),
            P(BOTH, None, None),
            P(BOTH, None, None),
            P(BOTH, None, None),
            P(BOTH, None),
            P(BOTH),
            P(BOTH, None),
            P(BOTH),
        ),
        out_specs=(P(BOTH, None, None), P(BOTH, None), P(BOTH)),
        check_vma=False,
    )
```

```python
import functools
import jax
import jax.numpy as jnp
import numpy as np
from jax import lax
from jax.experimental import pallas as pl
from jax.experimental.pallas import tpu as pltpu
from jax.sharding import PartitionSpec as P

learn_rate = 0.1
epsilon_value = 1e-08
CAP = 96
RP = 128
FIELD = 65536
BOTH = ("rows", "hst")
BF = jnp.bfloat16
F32 = jnp.float32
I32 = jnp.int32


def onehot(mask):
    return jnp.where(mask, 1.0, 0.0).astype(BF)


def iota(shape, dim):
    return lax.broadcasted_iota(I32, shape, dim)


def params(*sem):
    return pltpu.CompilerParams(dimension_semantics=sem or None)


def route_kernel(own_ref, slot_ref, bag_ref, w_ref, meta_ref, rank_ref, acc, base, upper):
    steps, k = own_ref.shape
    n = acc.shape[0]
    acc[...] = jnp.zeros_like(acc)
    base[...] = jnp.zeros_like(base)
    upper[...] = onehot(iota((k, k), 0) < iota((k, k), 1))

    def step(i, carry):
        row = pl.ds(i, 1)
        mask = iota((n, k), 0) == own_ref[row, :]
        a = onehot(mask)
        before = jnp.dot(a, upper[...], preferred_element_type=F32)
        start = jnp.concatenate([base[...]] * (k // RP), axis=1)
        rank = jnp.sum(jnp.where(mask, before + start, 0.0), axis=0, keepdims=True)
        base[...] += jnp.dot(a, jnp.ones((k, RP), BF), preferred_element_type=F32)
        rank = rank.astype(I32)
        rank_ref[row, :] = rank
        put = iota((RP, k), 0) == rank
        slot = slot_ref[row, :]
        parts = [
            (slot >> 8).astype(F32),
            (slot & 255).astype(F32),
            bag_ref[row, :].astype(F32),
            w_ref[row, :],
        ]
        b = jnp.concatenate([jnp.where(put, p, 0.0).astype(BF) for p in parts], axis=0)
        acc[...] += lax.dot_general(a, b, (((1,), (1,)), ((), ())), preferred_element_type=F32)
        return carry

    lax.fori_loop(0, steps, step, 0)
    slots = (acc[:, 0:RP] * 256.0 + acc[:, RP : 2 * RP]).astype(I32)
    meta_ref[:, 0, :] = slots * FIELD + acc[:, 2 * RP : 3 * RP].astype(I32)
    meta_ref[:, 1, :] = (acc[:, 3 * RP : 4 * RP] * float(FIELD)).astype(I32)


def spots(slot, k):
    hi = jnp.broadcast_to((slot >> 4).astype(F32), (16, k)).astype(BF)
    lo = jnp.broadcast_to((slot & 15).astype(F32), (16, k)).astype(BF)
    return hi, lo == iota((16, k), 0).astype(F32).astype(BF)


def tile_of(hi, base, first, count):
    zero = jnp.zeros_like(base)
    return jnp.concatenate(
        [jnp.where(hi == jnp.asarray(first + t, BF), base, zero) for t in range(count)], axis=0
    )


def owner_kernel(
    live_ref, count_ref, id_ref, w_ref, g_ref, table_ref, states_ref,
    prod_ref, new_table_ref, new_states_ref, tab, grad, hot,
):
    c = pl.program_id(0)
    touched, width = table_ref.shape
    k = id_ref.shape[2]
    bags = g_ref.shape[2]
    blocks = touched // 128

    @pl.when(c == 0)
    def _():
        grad[...] = jnp.zeros_like(grad)
        for m in range(blocks):
            t = table_ref[m * 128 : (m + 1) * 128, :].T
            high = t.astype(BF)
            tab[0:width, m * 128 : (m + 1) * 128] = high
            tab[width : 2 * width, m * 128 : (m + 1) * 128] = (t - high.astype(F32)).astype(BF)

    prod_ref[...] = jnp.zeros_like(prod_ref)

    def some(q, first, count):
        @pl.when(live_ref[c * 8 + q] != 0)
        def _():
            ids = id_ref[0, pl.ds(q, 1), :]
            per = k // count
            bag = (ids & (FIELD - 1)) + lax.broadcasted_iota(I32, (1, k), 1) // per * bags
            hi, at = spots(bag, k)
            one = jnp.where(at, jnp.ones((16, k), BF), jnp.zeros((16, k), BF))
            got = jnp.zeros((width, k), F32)
            for s in range(count):
                pick = tile_of(hi, one, bags // 16 * s, bags // 16)
                got += jnp.dot(g_ref[first + s], pick, preferred_element_type=F32)
            hi, at = spots(ids >> 16, k)
            w = w_ref[0, pl.ds(q, 1), :].astype(F32) * (1.0 / FIELD)
            w = jnp.broadcast_to(w, (16, k)).astype(BF)
            base = jnp.where(at, w, jnp.zeros_like(w))
            for m in range(touched // 256):
                hot[m * 256 : (m + 1) * 256, :] = tile_of(hi, base, 16 * m, 16)
            rows = jnp.dot(tab[...], hot[...], preferred_element_type=F32)
            rows = rows[0:width] + rows[width:]
            prod_ref[0, pl.ds(q, 1), :] = jnp.sum(rows * got, axis=0, keepdims=True)
            got = got.astype(BF)
            for m in range(touched // 256):
                at = slice(m * 256, (m + 1) * 256)
                grad[:, at] += lax.dot_general(
                    got, hot[at, :], (((1,), (1,)), ((), ())), preferred_element_type=F32
                )

    def low(q, carry):
        some(q, q * 4, 4)
        return carry

    def high_ranks(q, carry):
        some(q, 0, 16)
        return carry

    lax.fori_loop(0, 4, low, 0)
    lax.fori_loop(4, 6, high_ranks, 0)

    @pl.when(c == pl.num_programs(0) - 1)
    def _():
        for m in range(blocks):
            at = slice(m * 128, (m + 1) * 128)
            r = grad[:, at]
            summed = states_ref[m : m + 1, :] + jnp.mean(r * r, axis=0, keepdims=True)
            delta = learn_rate * r / (jnp.sqrt(summed) + epsilon_value)
            left = count_ref[0] - m * 128
            updated = table_ref[at, :] - delta.T
            new_table_ref[at, :] = jnp.where(iota((128, width), 0) < left, updated, 0.0)
            new_states_ref[m : m + 1, :] = jnp.where(iota((1, 128), 1) < left, summed, 0.0)


def back_kernel(own_ref, rank_ref, w_ref, prod_ref, out_ref, parts):
    steps, k = own_ref.shape
    n = prod_ref.shape[0]
    t = prod_ref[...].T
    high = t.astype(BF)
    rest = t - high.astype(F32)
    mid = rest.astype(BF)
    parts[0:RP, :] = high
    parts[RP : 2 * RP, :] = mid
    parts[2 * RP : 3 * RP, :] = (rest - mid.astype(F32)).astype(BF)

    def step(i, carry):
        row = pl.ds(i, 1)
        a = onehot(iota((n, k), 0) == own_ref[row, :])
        x = jnp.dot(parts[...], a, preferred_element_type=F32)
        x = (x[2 * RP :] + x[RP : 2 * RP]) + x[0:RP]
        x = jnp.where(iota((RP, k), 0) == rank_ref[row, :], x, 0.0)
        out_ref[row, :] = jnp.sum(x, axis=0, keepdims=True) / w_ref[row, :]
        return carry

    lax.fori_loop(0, steps, step, 0)


def local(grad_pooled, weights, owner, slot, lengths, counts, table, states):
    devices = lax.axis_size("rows") * lax.axis_size("hst")
    bags, features, per_bag = weights.shape
    width = grad_pooled.shape[2]
    touched = table.shape[0]
    total_ids = bags * features * per_bag
    n_bags = bags * features
    k1 = 256
    steps = total_ids // k1
    vmem = pl.BlockSpec(memory_space=pltpu.VMEM)
    live = jnp.arange(per_bag, dtype=I32)[None, None, :] < lengths[:, :, None]
    own = jnp.where(live, owner, -1).reshape(steps, k1)
    slots = slot.reshape(steps, k1)
    w = weights.astype(F32).reshape(steps, k1)
    bag = jnp.asarray((np.arange(total_ids) // per_bag).reshape(steps, k1), I32)
    g = grad_pooled.reshape(n_bags, width)

    everyone = lax.all_gather(g.T, BOTH, axis=0, tiled=False)
    meta, rank = pl.pallas_call(
        route_kernel,
        out_shape=(
            jax.ShapeDtypeStruct((devices, 2, RP), I32),
            jax.ShapeDtypeStruct((steps, k1), I32),
        ),
        in_specs=[vmem] * 4,
        out_specs=(vmem,) * 2,
        scratch_shapes=[
            pltpu.VMEM((devices, 4 * RP), F32),
            pltpu.VMEM((devices, RP), F32),
            pltpu.VMEM((k1, k1), BF),
        ],
        name="route",
    )(own, slots, bag, w)
    got_meta = lax.all_to_all(meta, BOTH, split_axis=0, concat_axis=0, tiled=True)

    srcs = 16
    groups = devices // srcs
    k2 = 256

    def in_rows(v):
        return jnp.concatenate(
            [
                v[:, 0:64].reshape(groups, 4, k2),
                v[:, 64:80].reshape(groups, 1, k2),
                v[:, 80:96].reshape(groups, 1, k2),
                jnp.zeros((groups, 2, k2), v.dtype),
            ],
            axis=1,
        )

    got_ids = in_rows(got_meta[:, 0, :])
    got_w = in_rows(got_meta[:, 1, :])
    active = (jnp.max(got_w, axis=2) > 0).astype(I32).reshape(-1)

    prods, new_table, new_states = pl.pallas_call(
        owner_kernel,
        grid_spec=pltpu.PrefetchScalarGridSpec(
            num_scalar_prefetch=2,
            grid=(groups,),
            in_specs=[
                pl.BlockSpec((1, 8, k2), lambda c, *_: (c, 0, 0)),
                pl.BlockSpec((1, 8, k2), lambda c, *_: (c, 0, 0)),
                pl.BlockSpec((srcs, width, n_bags), lambda c, *_: (c, 0, 0)),
                pl.BlockSpec((touched, width), lambda c, *_: (0, 0)),
                pl.BlockSpec((touched // 128, 128), lambda c, *_: (0, 0)),
            ],
            out_specs=(
                pl.BlockSpec((1, 8, k2), lambda c, *_: (c, 0, 0)),
                pl.BlockSpec((touched, width), lambda c, *_: (0, 0)),
                pl.BlockSpec((touched // 128, 128), lambda c, *_: (0, 0)),
            ),
            scratch_shapes=[
                pltpu.VMEM((2 * width, touched), BF),
                pltpu.VMEM((width, touched), F32),
                pltpu.VMEM((touched, k2), BF),
            ],
        ),
        out_shape=(
            jax.ShapeDtypeStruct((groups, 8, k2), F32),
            jax.ShapeDtypeStruct((touched, width), F32),
            jax.ShapeDtypeStruct((touched // 128, 128), F32),
        ),
        compiler_params=params("arbitrary"),
        name="owner_step",
    )(active, counts, got_ids, got_w, everyone, table, states.reshape(touched // 128, 128))

    back = jnp.concatenate(
        [
            prods[:, 0:4].reshape(devices, 64),
            prods[:, 4].reshape(devices, 16),
            prods[:, 5].reshape(devices, 16),
        ],
        axis=1,
    )
    back = jnp.pad(back, ((0, 0), (0, RP - CAP)))
    returned = lax.all_to_all(back, BOTH, split_axis=0, concat_axis=0, tiled=True)
    weight_grad = pl.pallas_call(
        back_kernel,
        out_shape=jax.ShapeDtypeStruct((steps, k1), F32),
        in_specs=[vmem] * 4,
        out_specs=vmem,
        scratch_shapes=[pltpu.VMEM((3 * RP, devices), BF)],
        name="back",
    )(own, rank, w, returned)
    return (weight_grad.reshape(weights.shape), new_table, new_states.reshape(-1))


def solution(mesh):
    return jax.shard_map(
        local,
        mesh=mesh,
        in_specs=(
            P(BOTH, None, None),
            P(BOTH, None, None),
            P(BOTH, None, None),
            P(BOTH, None, None),
            P(BOTH, None),
            P(BOTH),
            P(BOTH, None),
            P(BOTH),
        ),
        out_specs=(P(BOTH, None, None), P(BOTH, None), P(BOTH)),
        check_vma=False,
    )
```

```python
import functools
import jax
import jax.numpy as jnp
import numpy as np
from jax import lax
from jax.experimental import pallas as pl
from jax.experimental.pallas import tpu as pltpu
from jax.sharding import PartitionSpec as P

learn_rate = 0.1
epsilon_value = 1e-08
CAP = 96
RP = 128
FIELD = 65536
BOTH = ("rows", "hst")
BF = jnp.bfloat16
F32 = jnp.float32
I32 = jnp.int32


def onehot(mask):
    return jnp.where(mask, 1.0, 0.0).astype(BF)


def iota(shape, dim):
    return lax.broadcasted_iota(I32, shape, dim)


def params(*sem):
    return pltpu.CompilerParams(dimension_semantics=sem or None)


MESH = pl.DeviceIdType.MESH
PARTS = ((0, 32, "xyz"), (32, 48, "yzx"), (80, 48, "zxy"))
SIZE = {"x": 4, "y": 4, "z": 8}
STEPS = 8


def hops(order):
    return [(d, s) for d in order for s in range(SIZE[d] // 2)]


def copies_count():
    ring = 2 * STEPS * len(PARTS)
    return ring, ring + sum(1 + SIZE[order[2]] for _, _, order in PARTS)


class Spread:
    def __init__(self, own, out, send, recv, local):
        r = lax.axis_index("rows")
        self.me = {"x": r // 8, "y": (r // 2) % 4, "z": lax.axis_index("hst")}
        self.c = r % 2
        self.own, self.out, self.send, self.recv = own, out, send, recv
        self.used = 0
        self.started, self.pending = [], {}
        me = self.me
        self.local = pltpu.make_async_copy(
            own,
            out.at[pl.ds(me["x"], 1), pl.ds(me["y"], 1), pl.ds(self.c, 1), pl.ds(me["z"], 1)],
            local,
        )

    def device(self, d=None, by=0, core=None):
        at = dict(self.me)
        if d is not None:
            at[d] = (at[d] + by + SIZE[d]) % SIZE[d]
        c = self.c if core is None else core
        return ((at["x"] * 4 + at["y"]) * 2 + c, at["z"])

    def greet(self):
        barrier = pltpu.get_barrier_semaphore()
        near = [self.device(d, by) for d in "xyz" for by in (-1, 1)]
        for to in near + [self.device(core=1 - self.c)]:
            pl.semaphore_signal(barrier, inc=1, device_id=to, device_id_type=MESH)
        pl.semaphore_wait(barrier, 7)

    def region(self, part, d, by, half=None):
        first, count, order = PARTS[part]
        full = order[: order.index(d)]
        index = {}
        for e in "xyz":
            if e == d:
                index[e] = pl.ds((self.me[e] + by + SIZE[e]) % SIZE[e], 1)
            elif e in full:
                index[e] = pl.ds(0, SIZE[e])
            else:
                index[e] = pl.ds(self.me[e], 1)
        if half is not None:
            if full:
                n = SIZE[full[0]] // 2
                index[full[0]] = pl.ds(half * n, n)
            else:
                cut = (count + 31) // 32 * 16
                first, count = (first, cut) if half == 0 else (first + cut, count - cut)
        return self.out.at[
            index["x"], index["y"], pl.ds(self.c, 1), index["z"], pl.ds(first, count), :
        ]

    def copy(self, ref, to, src=None):
        i = self.used
        self.used += 1
        c = pltpu.make_async_remote_copy(
            src_ref=ref if src is None else src,
            dst_ref=ref,
            send_sem=self.send.at[i],
            recv_sem=self.recv.at[i],
            device_id=to,
            device_id_type=MESH,
        )
        c.start()
        self.started.append(c)
        return c

    def start(self, part, step, way):
        d, s = hops(PARTS[part][2])[step]
        last = s == SIZE[d] // 2 - 1
        half = None if not last else (0 if way == 1 else 1)
        ref = self.region(part, d, -way * s, half)
        first, count, _ = PARTS[part]
        src = self.own.at[:, :, :, :, pl.ds(first, count), :] if step == 0 else None
        copy = self.copy(ref, self.device(d, way), src)
        self.pending[part, way] = (copy, d, -way * (s + 1), half)

    def first(self):
        for part in range(len(PARTS)):
            for way in (1, -1):
                self.start(part, 0, way)

    def give(self, ref):
        self.given.append(self.copy(ref, self.device(core=1 - self.c)))

    def round(self, step):
        if step == 0:
            self.given = []
        for part, (_, _, order) in enumerate(PARTS):
            plan = hops(order)
            d, s = plan[step]
            more = step + 1 < STEPS
            same = more and plan[step + 1][0] == d
            got = []
            for way in (1, -1):
                copy, _, by, half = self.pending[part, way]
                copy.wait_recv()
                got.append((by, half))
                if same:
                    self.start(part, step + 1, way)
            if more and not same:
                for way in (1, -1):
                    self.start(part, step + 1, way)
                if plan[step + 1][0] == order[2]:
                    self.give(self.region(part, order[2], 0))
            if d == order[2]:
                for by, half in got:
                    self.give(self.region(part, d, by, half))

    def finish(self):
        for c in self.given:
            c.wait_recv()
        for c in self.started:
            c.wait_send()


def route_kernel(
    own_ref, slot_ref, bag_ref, w_ref, block_ref,
    meta_ref, rank_ref, everyone_ref,
    acc, base, upper, send, recv, placed,
):
    spread = Spread(block_ref, everyone_ref, send, recv, placed)
    spread.greet()
    spread.local.start()
    spread.first()
    steps, k = own_ref.shape
    n = acc.shape[0]
    acc[...] = jnp.zeros_like(acc)
    base[...] = jnp.zeros_like(base)
    upper[...] = onehot(iota((k, k), 0) < iota((k, k), 1))

    def step(i, carry):
        row = pl.ds(i, 1)
        mask = iota((n, k), 0) == own_ref[row, :]
        a = onehot(mask)
        before = jnp.dot(a, upper[...], preferred_element_type=F32)
        start = jnp.concatenate([base[...]] * (k // RP), axis=1)
        rank = jnp.sum(jnp.where(mask, before + start, 0.0), axis=0, keepdims=True)
        base[...] += jnp.dot(a, jnp.ones((k, RP), BF), preferred_element_type=F32)
        rank = rank.astype(I32)
        rank_ref[row, :] = rank
        put = iota((RP, k), 0) == rank
        slot = slot_ref[row, :]
        parts = [
            (slot >> 8).astype(F32),
            (slot & 255).astype(F32),
            bag_ref[row, :].astype(F32),
            w_ref[row, :],
        ]
        b = jnp.concatenate([jnp.where(put, p, 0.0).astype(BF) for p in parts], axis=0)
        acc[...] += lax.dot_general(a, b, (((1,), (1,)), ((), ())), preferred_element_type=F32)
        return carry

    done = 0
    for i in range(STEPS):
        upto = (i + 1) * steps // 14 if i < 4 else steps - (STEPS - 1 - i) * steps // 6
        lax.fori_loop(done, upto, step, 0)
        done = upto
        if i == 0:
            spread.local.wait()
        spread.round(i)
    slots = (acc[:, 0:RP] * 256.0 + acc[:, RP : 2 * RP]).astype(I32)
    meta_ref[:, 0, :] = slots * FIELD + acc[:, 2 * RP : 3 * RP].astype(I32)
    meta_ref[:, 1, :] = (acc[:, 3 * RP : 4 * RP] * float(FIELD)).astype(I32)
    spread.finish()


def spots(slot, k):
    hi = jnp.broadcast_to((slot >> 4).astype(F32), (16, k)).astype(BF)
    lo = jnp.broadcast_to((slot & 15).astype(F32), (16, k)).astype(BF)
    return hi, lo == iota((16, k), 0).astype(F32).astype(BF)


def tile_of(hi, base, first, count):
    zero = jnp.zeros_like(base)
    return jnp.concatenate(
        [jnp.where(hi == jnp.asarray(first + t, BF), base, zero) for t in range(count)], axis=0
    )


def owner_kernel(
    live_ref, count_ref, id_ref, w_ref, g_ref, table_ref, states_ref,
    prod_ref, new_table_ref, new_states_ref, tab, grad, hot,
):
    c = pl.program_id(0)
    touched, width = table_ref.shape
    k = id_ref.shape[2]
    bags = g_ref.shape[2]
    blocks = touched // 128

    @pl.when(c == 0)
    def _():
        grad[...] = jnp.zeros_like(grad)
        for m in range(blocks):
            t = table_ref[m * 128 : (m + 1) * 128, :].T
            high = t.astype(BF)
            tab[0:width, m * 128 : (m + 1) * 128] = high
            tab[width : 2 * width, m * 128 : (m + 1) * 128] = (t - high.astype(F32)).astype(BF)

    prod_ref[...] = jnp.zeros_like(prod_ref)

    def some(q, first, count):
        @pl.when(live_ref[c * 8 + q] != 0)
        def _():
            ids = id_ref[0, pl.ds(q, 1), :]
            per = k // count
            bag = (ids & (FIELD - 1)) + lax.broadcasted_iota(I32, (1, k), 1) // per * bags
            hi, at = spots(bag, k)
            one = jnp.where(at, jnp.ones((16, k), BF), jnp.zeros((16, k), BF))
            got = jnp.zeros((width, k), F32)
            for s in range(count):
                pick = tile_of(hi, one, bags // 16 * s, bags // 16)
                got += jnp.dot(g_ref[first + s], pick, preferred_element_type=F32)
            hi, at = spots(ids >> 16, k)
            w = w_ref[0, pl.ds(q, 1), :].astype(F32) * (1.0 / FIELD)
            w = jnp.broadcast_to(w, (16, k)).astype(BF)
            base = jnp.where(at, w, jnp.zeros_like(w))
            for m in range(touched // 256):
                hot[m * 256 : (m + 1) * 256, :] = tile_of(hi, base, 16 * m, 16)
            rows = jnp.dot(tab[...], hot[...], preferred_element_type=F32)
            rows = rows[0:width] + rows[width:]
            prod_ref[0, pl.ds(q, 1), :] = jnp.sum(rows * got, axis=0, keepdims=True)
            got = got.astype(BF)
            for m in range(touched // 256):
                at = slice(m * 256, (m + 1) * 256)
                grad[:, at] += lax.dot_general(
                    got, hot[at, :], (((1,), (1,)), ((), ())), preferred_element_type=F32
                )

    def low(q, carry):
        some(q, q * 4, 4)
        return carry

    def high_ranks(q, carry):
        some(q, 0, 16)
        return carry

    lax.fori_loop(0, 4, low, 0)
    lax.fori_loop(4, 6, high_ranks, 0)

    @pl.when(c == pl.num_programs(0) - 1)
    def _():
        for m in range(blocks):
            at = slice(m * 128, (m + 1) * 128)
            r = grad[:, at]
            summed = states_ref[m : m + 1, :] + jnp.mean(r * r, axis=0, keepdims=True)
            delta = learn_rate * r / (jnp.sqrt(summed) + epsilon_value)
            left = count_ref[0] - m * 128
            updated = table_ref[at, :] - delta.T
            new_table_ref[at, :] = jnp.where(iota((128, width), 0) < left, updated, 0.0)
            new_states_ref[m : m + 1, :] = jnp.where(iota((1, 128), 1) < left, summed, 0.0)


def back_kernel(own_ref, rank_ref, w_ref, prod_ref, out_ref, parts):
    steps, k = own_ref.shape
    n = prod_ref.shape[0]
    t = prod_ref[...].T
    high = t.astype(BF)
    rest = t - high.astype(F32)
    mid = rest.astype(BF)
    parts[0:RP, :] = high
    parts[RP : 2 * RP, :] = mid
    parts[2 * RP : 3 * RP, :] = (rest - mid.astype(F32)).astype(BF)

    def step(i, carry):
        row = pl.ds(i, 1)
        a = onehot(iota((n, k), 0) == own_ref[row, :])
        x = jnp.dot(parts[...], a, preferred_element_type=F32)
        x = (x[2 * RP :] + x[RP : 2 * RP]) + x[0:RP]
        x = jnp.where(iota((RP, k), 0) == rank_ref[row, :], x, 0.0)
        out_ref[row, :] = jnp.sum(x, axis=0, keepdims=True) / w_ref[row, :]
        return carry

    lax.fori_loop(0, steps, step, 0)


def local(grad_pooled, weights, owner, slot, lengths, counts, table, states):
    devices = lax.axis_size("rows") * lax.axis_size("hst")
    bags, features, per_bag = weights.shape
    width = grad_pooled.shape[2]
    touched = table.shape[0]
    total_ids = bags * features * per_bag
    n_bags = bags * features
    k1 = 256
    steps = total_ids // k1
    vmem = pl.BlockSpec(memory_space=pltpu.VMEM)
    live = jnp.arange(per_bag, dtype=I32)[None, None, :] < lengths[:, :, None]
    own = jnp.where(live, owner, -1).reshape(steps, k1)
    slots = slot.reshape(steps, k1)
    w = weights.astype(F32).reshape(steps, k1)
    bag = jnp.asarray((np.arange(total_ids) // per_bag).reshape(steps, k1), I32)
    g = grad_pooled.reshape(n_bags, width)

    flights = copies_count()[1]
    meta, rank, everyone = pl.pallas_call(
        route_kernel,
        out_shape=(
            jax.ShapeDtypeStruct((devices, 2, RP), I32),
            jax.ShapeDtypeStruct((steps, k1), I32),
            jax.ShapeDtypeStruct((4, 4, 2, 8, width, n_bags), BF),
        ),
        in_specs=[vmem] * 5,
        out_specs=(vmem, vmem, pl.BlockSpec(memory_space=pl.ANY)),
        scratch_shapes=[
            pltpu.VMEM((devices, 4 * RP), F32),
            pltpu.VMEM((devices, RP), F32),
            pltpu.VMEM((k1, k1), BF),
            pltpu.SemaphoreType.DMA((flights,)),
            pltpu.SemaphoreType.DMA((flights,)),
            pltpu.SemaphoreType.DMA,
        ],
        compiler_params=pltpu.CompilerParams(collective_id=0, has_side_effects=True),
        name="route",
    )(own, slots, bag, w, g.T.reshape(1, 1, 1, 1, width, n_bags))
    everyone = everyone.reshape(devices, width, n_bags)
    got_meta = lax.all_to_all(meta, BOTH, split_axis=0, concat_axis=0, tiled=True)

    srcs = 16
    groups = devices // srcs
    k2 = 256

    def in_rows(v):
        return jnp.concatenate(
            [
                v[:, 0:64].reshape(groups, 4, k2),
                v[:, 64:80].reshape(groups, 1, k2),
                v[:, 80:96].reshape(groups, 1, k2),
                jnp.zeros((groups, 2, k2), v.dtype),
            ],
            axis=1,
        )

    got_ids = in_rows(got_meta[:, 0, :])
    got_w = in_rows(got_meta[:, 1, :])
    active = (jnp.max(got_w, axis=2) > 0).astype(I32).reshape(-1)

    prods, new_table, new_states = pl.pallas_call(
        owner_kernel,
        grid_spec=pltpu.PrefetchScalarGridSpec(
            num_scalar_prefetch=2,
            grid=(groups,),
            in_specs=[
                pl.BlockSpec((1, 8, k2), lambda c, *_: (c, 0, 0)),
                pl.BlockSpec((1, 8, k2), lambda c, *_: (c, 0, 0)),
                pl.BlockSpec((srcs, width, n_bags), lambda c, *_: (c, 0, 0)),
                pl.BlockSpec((touched, width), lambda c, *_: (0, 0)),
                pl.BlockSpec((touched // 128, 128), lambda c, *_: (0, 0)),
            ],
            out_specs=(
                pl.BlockSpec((1, 8, k2), lambda c, *_: (c, 0, 0)),
                pl.BlockSpec((touched, width), lambda c, *_: (0, 0)),
                pl.BlockSpec((touched // 128, 128), lambda c, *_: (0, 0)),
            ),
            scratch_shapes=[
                pltpu.VMEM((2 * width, touched), BF),
                pltpu.VMEM((width, touched), F32),
                pltpu.VMEM((touched, k2), BF),
            ],
        ),
        out_shape=(
            jax.ShapeDtypeStruct((groups, 8, k2), F32),
            jax.ShapeDtypeStruct((touched, width), F32),
            jax.ShapeDtypeStruct((touched // 128, 128), F32),
        ),
        compiler_params=params("arbitrary"),
        name="owner_step",
    )(active, counts, got_ids, got_w, everyone, table, states.reshape(touched // 128, 128))

    back = jnp.concatenate(
        [
            prods[:, 0:4].reshape(devices, 64),
            prods[:, 4].reshape(devices, 16),
            prods[:, 5].reshape(devices, 16),
        ],
        axis=1,
    )
    back = jnp.pad(back, ((0, 0), (0, RP - CAP)))
    returned = lax.all_to_all(back, BOTH, split_axis=0, concat_axis=0, tiled=True)
    weight_grad = pl.pallas_call(
        back_kernel,
        out_shape=jax.ShapeDtypeStruct((steps, k1), F32),
        in_specs=[vmem] * 4,
        out_specs=vmem,
        scratch_shapes=[pltpu.VMEM((3 * RP, devices), BF)],
        name="back",
    )(own, rank, w, returned)
    return (weight_grad.reshape(weights.shape), new_table, new_states.reshape(-1))


def solution(mesh):
    return jax.shard_map(
        local,
        mesh=mesh,
        in_specs=(
            P(BOTH, None, None),
            P(BOTH, None, None),
            P(BOTH, None, None),
            P(BOTH, None, None),
            P(BOTH, None),
            P(BOTH),
            P(BOTH, None),
            P(BOTH),
        ),
        out_specs=(P(BOTH, None, None), P(BOTH, None), P(BOTH)),
        check_vma=False,
    )
```

```python
import functools
import jax
import jax.numpy as jnp
import numpy as np
from jax import lax
from jax.experimental import pallas as pl
from jax.experimental.pallas import tpu as pltpu
from jax.sharding import PartitionSpec as P

learn_rate = 0.1
epsilon_value = 1e-08
CAP = 96
RP = 128
FIELD = 65536
BOTH = ("rows", "hst")
BF = jnp.bfloat16
F32 = jnp.float32
I32 = jnp.int32


def onehot(mask):
    return jnp.where(mask, 1.0, 0.0).astype(BF)


def iota(shape, dim):
    return lax.broadcasted_iota(I32, shape, dim)


def params(*sem):
    return pltpu.CompilerParams(dimension_semantics=sem or None)


MESH = pl.DeviceIdType.MESH
PARTS = ((0, 32, "xyz"), (32, 48, "zyx"), (80, 48, "zxy"))
SIZE = {"x": 4, "y": 4, "z": 8}
TURNS = (0, 0, 1, 2, 0, 0, 1, 2, 1, 2, 0, 0, 0, 1, 2, 0, 1, 2)
WORK = (2, 3, 2, 0, 1, 3, 2, 0, 4, 0, 6, 17, 0, 0, 0, 0, 0, 0)


def plan(order):
    ring = [(d, s) for d in order for s in range(SIZE[d] // 2)]
    return [("z", None)] + ring[SIZE["z"] // 2 :] if order[0] == "z" else ring


def copies_count():
    total = 0
    for _, _, order in PARTS:
        total += sum(SIZE["z"] - 1 if s is None else 2 for _, s in plan(order)) + 1 + SIZE[order[2]]
    return total


class Spread:
    def __init__(self, own, out, send, recv, local):
        r = lax.axis_index("rows")
        self.me = {"x": r // 8, "y": (r // 2) % 4, "z": lax.axis_index("hst")}
        self.c = r % 2
        self.own, self.out, self.send, self.recv = own, out, send, recv
        self.used = 0
        self.started, self.given = [], []
        self.step = [0] * len(PARTS)
        self.pending = [None] * len(PARTS)
        me = self.me
        self.local = pltpu.make_async_copy(
            own,
            out.at[pl.ds(me["x"], 1), pl.ds(me["y"], 1), pl.ds(self.c, 1), pl.ds(me["z"], 1)],
            local,
        )

    def device(self, d=None, by=0, core=None):
        at = dict(self.me)
        if d is not None:
            at[d] = (at[d] + by + SIZE[d]) % SIZE[d]
        c = self.c if core is None else core
        return ((at["x"] * 4 + at["y"]) * 2 + c, at["z"])

    def region(self, part, d, by, half=None):
        first, count, order = PARTS[part]
        full = order[: order.index(d)]
        index = {}
        for e in "xyz":
            if e == d:
                index[e] = pl.ds((self.me[e] + by + SIZE[e]) % SIZE[e], 1)
            elif e in full:
                index[e] = pl.ds(0, SIZE[e])
            else:
                index[e] = pl.ds(self.me[e], 1)
        if half is not None:
            if full:
                n = SIZE[full[0]] // 2
                index[full[0]] = pl.ds(half * n, n)
            else:
                cut = (count + 31) // 32 * 16
                first, count = (first, cut) if half == 0 else (first + cut, count - cut)
        return self.out.at[
            index["x"], index["y"], pl.ds(self.c, 1), index["z"], pl.ds(first, count), :
        ]

    def copy(self, ref, to, src=None):
        i = self.used
        self.used += 1
        c = pltpu.make_async_remote_copy(
            src_ref=ref if src is None else src,
            dst_ref=ref,
            send_sem=self.send.at[i],
            recv_sem=self.recv.at[i],
            device_id=to,
            device_id_type=MESH,
        )
        c.start()
        self.started.append(c)
        return c

    def start(self, part, step, way):
        first, count, order = PARTS[part]
        d, s = plan(order)[step]
        src = self.own.at[:, :, :, :, pl.ds(first, count), :] if step == 0 else None
        if s is None:
            return self.copy(self.region(part, d, 0), self.device(d, way), src), -way, None
        half = None if s < SIZE[d] // 2 - 1 else (0 if way == 1 else 1)
        ref = self.region(part, d, -way * s, half)
        return self.copy(ref, self.device(d, way), src), -way * (s + 1), half

    def ways(self, part):
        _, s = plan(PARTS[part][2])[self.step[part]]
        return range(1, SIZE["z"]) if s is None else (1, -1)

    def first(self):
        for part in range(len(PARTS)):
            self.pending[part] = [self.start(part, 0, way) for way in self.ways(part)]

    def give(self, ref):
        self.given.append(self.copy(ref, self.device(core=1 - self.c)))

    def turn(self, part):
        order = PARTS[part][2]
        steps = plan(order)
        step = self.step[part]
        d, s = steps[step]
        more = step + 1 < len(steps)
        same = more and steps[step + 1][0] == d
        arrived, self.pending[part] = self.pending[part], []
        self.step[part] += 1
        for i, (copy, _, _) in enumerate(arrived):
            copy.wait_recv()
            if same:
                self.pending[part].append(self.start(part, step + 1, (1, -1)[i]))
        if more and not same:
            self.pending[part] = [self.start(part, step + 1, way) for way in self.ways(part)]
            if steps[step + 1][0] == order[2]:
                self.give(self.region(part, order[2], 0))
        if d == order[2]:
            for _, by, half in arrived:
                self.give(self.region(part, d, by, half))

    def finish(self):
        for c in self.given:
            c.wait_recv()
        for c in self.started:
            c.wait_send()


ROWS, HST = 32, 8
PEERS = HST - 1 + ROWS - 1


def greet_all():
    r, z = lax.axis_index("rows"), lax.axis_index("hst")
    barrier = pltpu.get_barrier_semaphore()
    for k in range(1, HST):
        pl.semaphore_signal(barrier, inc=1, device_id=(r, (z + k) % HST), device_id_type=MESH)

    def tell(k, carry):
        pl.semaphore_signal(barrier, inc=1, device_id=((r + k) % ROWS, z), device_id_type=MESH)
        return carry

    lax.fori_loop(1, ROWS, tell, 0)
    pl.semaphore_wait(barrier, PEERS)


class Exchange:
    def __init__(self, src, mid, dst, send, recv):
        self.r, self.z = lax.axis_index("rows"), lax.axis_index("hst")
        self.src, self.mid, self.dst, self.send, self.recv = src, mid, dst, send, recv

    def down(self, k):
        return pltpu.make_async_remote_copy(
            src_ref=self.src.at[:, pl.ds((self.z + k) % HST, 1)],
            dst_ref=self.mid.at[:, pl.ds(self.z, 1)],
            send_sem=self.send.at[k - 1],
            recv_sem=self.recv.at[k - 1],
            device_id=(self.r, (self.z + k) % HST),
            device_id_type=MESH,
        )

    def across(self, k):
        to = (self.r + k) % ROWS
        return pltpu.make_async_remote_copy(
            src_ref=self.mid.at[pl.ds(to, 1)],
            dst_ref=self.dst.at[pl.ds(self.r, 1)],
            send_sem=self.send.at[HST - 2 + k],
            recv_sem=self.recv.at[HST - 2 + k],
            device_id=(to, self.z),
            device_id_type=MESH,
        )

    def each(self, first, last, act):
        def body(k, carry):
            act(k)
            return carry

        lax.fori_loop(first, last, body, 0)

    def begin(self):
        self.each(1, HST, lambda k: self.down(k).start())
        self.mid[:, pl.ds(self.z, 1)] = self.src[:, pl.ds(self.z, 1)]

    def turn(self):
        self.each(1, HST, lambda k: self.down(k).wait_recv())
        self.each(1, ROWS, lambda k: self.across(k).start())
        self.dst[pl.ds(self.r, 1)] = self.mid[pl.ds(self.r, 1)]

    def finish(self):
        self.each(1, ROWS, lambda k: self.across(k).wait_recv())
        self.each(1, HST, lambda k: self.down(k).wait_send())
        self.each(1, ROWS, lambda k: self.across(k).wait_send())


def route_kernel(
    own_ref, slot_ref, bag_ref, w_ref, block_ref,
    got_ref, rank_ref, everyone_ref,
    acc, base, upper, meta_ref, mid_ref, send, recv, placed, meta_send, meta_recv,
):
    greet_all()
    spread = Spread(block_ref, everyone_ref, send, recv, placed)
    spread.local.start()
    spread.first()
    steps, k = own_ref.shape
    n = acc.shape[0]
    acc[...] = jnp.zeros_like(acc)
    base[...] = jnp.zeros_like(base)
    upper[...] = onehot(iota((k, k), 0) < iota((k, k), 1))

    def step(i, carry):
        row = pl.ds(i, 1)
        mask = iota((n, k), 0) == own_ref[row, :]
        a = onehot(mask)
        before = jnp.dot(a, upper[...], preferred_element_type=F32)
        start = jnp.concatenate([base[...]] * (k // RP), axis=1)
        rank = jnp.sum(jnp.where(mask, before + start, 0.0), axis=0, keepdims=True)
        base[...] += jnp.dot(a, jnp.ones((k, RP), BF), preferred_element_type=F32)
        rank = rank.astype(I32)
        rank_ref[row, :] = rank
        put = iota((RP, k), 0) == rank
        slot = slot_ref[row, :]
        parts = [
            (slot >> 8).astype(F32),
            (slot & 255).astype(F32),
            bag_ref[row, :].astype(F32),
            w_ref[row, :],
        ]
        b = jnp.concatenate([jnp.where(put, p, 0.0).astype(BF) for p in parts], axis=0)
        acc[...] += lax.dot_general(a, b, (((1,), (1,)), ((), ())), preferred_element_type=F32)
        return carry

    exchange = Exchange(meta_ref, mid_ref, got_ref, meta_send, meta_recv)
    done = 0
    for i, (part, work) in enumerate(zip(TURNS, WORK)):
        if work:
            upto = steps if i == 11 else done + work
            lax.fori_loop(done, upto, step, 0)
            done = upto
        if i == 0:
            spread.local.wait()
        if i == 12:
            slots = (acc[:, 0:RP] * 256.0 + acc[:, RP : 2 * RP]).astype(I32)
            ids = slots * FIELD + acc[:, 2 * RP : 3 * RP].astype(I32)
            meta_ref[:, :, 0, :] = ids.reshape(ROWS, HST, RP)
            codes = (acc[:, 3 * RP : 4 * RP] * float(FIELD)).astype(I32)
            meta_ref[:, :, 1, :] = codes.reshape(ROWS, HST, RP)
            exchange.begin()
        if i == 13:
            exchange.turn()
        spread.turn(part)
    exchange.finish()
    spread.finish()


def spots(slot, k):
    hi = jnp.broadcast_to((slot >> 4).astype(F32), (16, k)).astype(BF)
    lo = jnp.broadcast_to((slot & 15).astype(F32), (16, k)).astype(BF)
    return hi, lo == iota((16, k), 0).astype(F32).astype(BF)


def tile_of(hi, base, first, count):
    zero = jnp.zeros_like(base)
    return jnp.concatenate(
        [jnp.where(hi == jnp.asarray(first + t, BF), base, zero) for t in range(count)], axis=0
    )


def owner_kernel(
    live_ref, count_ref, id_ref, w_ref, g_ref, table_ref, states_ref,
    prod_ref, new_table_ref, new_states_ref, tab, grad, hot,
):
    c = pl.program_id(0)
    touched, width = table_ref.shape
    k = id_ref.shape[2]
    bags = g_ref.shape[2]
    blocks = touched // 128

    @pl.when(c == 0)
    def _():
        grad[...] = jnp.zeros_like(grad)
        for m in range(blocks):
            t = table_ref[m * 128 : (m + 1) * 128, :].T
            high = t.astype(BF)
            tab[0:width, m * 128 : (m + 1) * 128] = high
            tab[width : 2 * width, m * 128 : (m + 1) * 128] = (t - high.astype(F32)).astype(BF)

    prod_ref[...] = jnp.zeros_like(prod_ref)

    def some(q, first, count):
        @pl.when(live_ref[c * 8 + q] != 0)
        def _():
            ids = id_ref[0, pl.ds(q, 1), :]
            per = k // count
            bag = (ids & (FIELD - 1)) + lax.broadcasted_iota(I32, (1, k), 1) // per * bags
            hi, at = spots(bag, k)
            one = jnp.where(at, jnp.ones((16, k), BF), jnp.zeros((16, k), BF))
            got = jnp.zeros((width, k), F32)
            for s in range(count):
                pick = tile_of(hi, one, bags // 16 * s, bags // 16)
                got += jnp.dot(g_ref[first + s], pick, preferred_element_type=F32)
            hi, at = spots(ids >> 16, k)
            w = w_ref[0, pl.ds(q, 1), :].astype(F32) * (1.0 / FIELD)
            w = jnp.broadcast_to(w, (16, k)).astype(BF)
            base = jnp.where(at, w, jnp.zeros_like(w))
            for m in range(touched // 256):
                hot[m * 256 : (m + 1) * 256, :] = tile_of(hi, base, 16 * m, 16)
            rows = jnp.dot(tab[...], hot[...], preferred_element_type=F32)
            rows = rows[0:width] + rows[width:]
            prod_ref[0, pl.ds(q, 1), :] = jnp.sum(rows * got, axis=0, keepdims=True)
            got = got.astype(BF)
            for m in range(touched // 256):
                at = slice(m * 256, (m + 1) * 256)
                grad[:, at] += lax.dot_general(
                    got, hot[at, :], (((1,), (1,)), ((), ())), preferred_element_type=F32
                )

    def low(q, carry):
        some(q, q * 4, 4)
        return carry

    def high_ranks(q, carry):
        some(q, 0, 16)
        return carry

    lax.fori_loop(0, 4, low, 0)
    lax.fori_loop(4, 6, high_ranks, 0)

    @pl.when(c == pl.num_programs(0) - 1)
    def _():
        for m in range(blocks):
            at = slice(m * 128, (m + 1) * 128)
            r = grad[:, at]
            summed = states_ref[m : m + 1, :] + jnp.mean(r * r, axis=0, keepdims=True)
            delta = learn_rate * r / (jnp.sqrt(summed) + epsilon_value)
            left = count_ref[0] - m * 128
            updated = table_ref[at, :] - delta.T
            new_table_ref[at, :] = jnp.where(iota((128, width), 0) < left, updated, 0.0)
            new_states_ref[m : m + 1, :] = jnp.where(iota((1, 128), 1) < left, summed, 0.0)


def back_kernel(own_ref, rank_ref, w_ref, prod_ref, out_ref, parts):
    steps, k = own_ref.shape
    n = prod_ref.shape[0]
    t = prod_ref[...].T
    high = t.astype(BF)
    rest = t - high.astype(F32)
    mid = rest.astype(BF)
    parts[0:RP, :] = high
    parts[RP : 2 * RP, :] = mid
    parts[2 * RP : 3 * RP, :] = (rest - mid.astype(F32)).astype(BF)

    def step(i, carry):
        row = pl.ds(i, 1)
        a = onehot(iota((n, k), 0) == own_ref[row, :])
        x = jnp.dot(parts[...], a, preferred_element_type=F32)
        x = (x[2 * RP :] + x[RP : 2 * RP]) + x[0:RP]
        x = jnp.where(iota((RP, k), 0) == rank_ref[row, :], x, 0.0)
        out_ref[row, :] = jnp.sum(x, axis=0, keepdims=True) / w_ref[row, :]
        return carry

    lax.fori_loop(0, steps, step, 0)


def local(grad_pooled, weights, owner, slot, lengths, counts, table, states):
    devices = lax.axis_size("rows") * lax.axis_size("hst")
    bags, features, per_bag = weights.shape
    width = grad_pooled.shape[2]
    touched = table.shape[0]
    total_ids = bags * features * per_bag
    n_bags = bags * features
    k1 = 256
    steps = total_ids // k1
    vmem = pl.BlockSpec(memory_space=pltpu.VMEM)
    live = jnp.arange(per_bag, dtype=I32)[None, None, :] < lengths[:, :, None]
    own = jnp.where(live, owner, -1).reshape(steps, k1)
    slots = slot.reshape(steps, k1)
    w = weights.astype(F32).reshape(steps, k1)
    bag = jnp.asarray((np.arange(total_ids) // per_bag).reshape(steps, k1), I32)
    g = grad_pooled.reshape(n_bags, width)

    flights = copies_count()
    got_meta, rank, everyone = pl.pallas_call(
        route_kernel,
        out_shape=(
            jax.ShapeDtypeStruct((ROWS, HST, 2, RP), I32),
            jax.ShapeDtypeStruct((steps, k1), I32),
            jax.ShapeDtypeStruct((4, 4, 2, 8, width, n_bags), BF),
        ),
        in_specs=[vmem] * 5,
        out_specs=(vmem, vmem, pl.BlockSpec(memory_space=pl.ANY)),
        scratch_shapes=[
            pltpu.VMEM((devices, 4 * RP), F32),
            pltpu.VMEM((devices, RP), F32),
            pltpu.VMEM((k1, k1), BF),
            pltpu.VMEM((ROWS, HST, 2, RP), I32),
            pltpu.VMEM((ROWS, HST, 2, RP), I32),
            pltpu.SemaphoreType.DMA((flights,)),
            pltpu.SemaphoreType.DMA((flights,)),
            pltpu.SemaphoreType.DMA,
            pltpu.SemaphoreType.DMA((PEERS,)),
            pltpu.SemaphoreType.DMA((PEERS,)),
        ],
        compiler_params=pltpu.CompilerParams(collective_id=0, has_side_effects=True),
        name="route",
    )(own, slots, bag, w, g.T.reshape(1, 1, 1, 1, width, n_bags))
    everyone = everyone.reshape(devices, width, n_bags)
    got_meta = got_meta.reshape(devices, 2, RP)

    srcs = 16
    groups = devices // srcs
    k2 = 256

    def in_rows(v):
        return jnp.concatenate(
            [
                v[:, 0:64].reshape(groups, 4, k2),
                v[:, 64:80].reshape(groups, 1, k2),
                v[:, 80:96].reshape(groups, 1, k2),
                jnp.zeros((groups, 2, k2), v.dtype),
            ],
            axis=1,
        )

    got_ids = in_rows(got_meta[:, 0, :])
    got_w = in_rows(got_meta[:, 1, :])
    active = (jnp.max(got_w, axis=2) > 0).astype(I32).reshape(-1)

    prods, new_table, new_states = pl.pallas_call(
        owner_kernel,
        grid_spec=pltpu.PrefetchScalarGridSpec(
            num_scalar_prefetch=2,
            grid=(groups,),
            in_specs=[
                pl.BlockSpec((1, 8, k2), lambda c, *_: (c, 0, 0)),
                pl.BlockSpec((1, 8, k2), lambda c, *_: (c, 0, 0)),
                pl.BlockSpec((srcs, width, n_bags), lambda c, *_: (c, 0, 0)),
                pl.BlockSpec((touched, width), lambda c, *_: (0, 0)),
                pl.BlockSpec((touched // 128, 128), lambda c, *_: (0, 0)),
            ],
            out_specs=(
                pl.BlockSpec((1, 8, k2), lambda c, *_: (c, 0, 0)),
                pl.BlockSpec((touched, width), lambda c, *_: (0, 0)),
                pl.BlockSpec((touched // 128, 128), lambda c, *_: (0, 0)),
            ),
            scratch_shapes=[
                pltpu.VMEM((2 * width, touched), BF),
                pltpu.VMEM((width, touched), F32),
                pltpu.VMEM((touched, k2), BF),
            ],
        ),
        out_shape=(
            jax.ShapeDtypeStruct((groups, 8, k2), F32),
            jax.ShapeDtypeStruct((touched, width), F32),
            jax.ShapeDtypeStruct((touched // 128, 128), F32),
        ),
        compiler_params=params("arbitrary"),
        name="owner_step",
    )(active, counts, got_ids, got_w, everyone, table, states.reshape(touched // 128, 128))

    back = jnp.concatenate(
        [
            prods[:, 0:4].reshape(devices, 64),
            prods[:, 4].reshape(devices, 16),
            prods[:, 5].reshape(devices, 16),
        ],
        axis=1,
    )
    back = jnp.pad(back, ((0, 0), (0, RP - CAP)))
    returned = lax.all_to_all(back, BOTH, split_axis=0, concat_axis=0, tiled=True)
    weight_grad = pl.pallas_call(
        back_kernel,
        out_shape=jax.ShapeDtypeStruct((steps, k1), F32),
        in_specs=[vmem] * 4,
        out_specs=vmem,
        scratch_shapes=[pltpu.VMEM((3 * RP, devices), BF)],
        name="back",
    )(own, rank, w, returned)
    return (weight_grad.reshape(weights.shape), new_table, new_states.reshape(-1))


def solution(mesh):
    return jax.shard_map(
        local,
        mesh=mesh,
        in_specs=(
            P(BOTH, None, None),
            P(BOTH, None, None),
            P(BOTH, None, None),
            P(BOTH, None, None),
            P(BOTH, None),
            P(BOTH),
            P(BOTH, None),
            P(BOTH),
        ),
        out_specs=(P(BOTH, None, None), P(BOTH, None), P(BOTH)),
        check_vma=False,
    )
```

```python
import functools
import jax
import jax.numpy as jnp
import numpy as np
from jax import lax
from jax.experimental import pallas as pl
from jax.experimental.pallas import tpu as pltpu
from jax.sharding import PartitionSpec as P

learn_rate = 0.1
epsilon_value = 1e-08
CAP = 96
RP = 128
FIELD = 65536
BOTH = ("rows", "hst")
BF = jnp.bfloat16
F32 = jnp.float32
I32 = jnp.int32


def onehot(mask):
    return jnp.where(mask, 1.0, 0.0).astype(BF)


def iota(shape, dim):
    return lax.broadcasted_iota(I32, shape, dim)


def params(*sem):
    return pltpu.CompilerParams(dimension_semantics=sem or None)


MESH = pl.DeviceIdType.MESH
PARTS = ((0, 32, "xyz"), (32, 48, "zyx"), (80, 48, "zxy"))
SIZE = {"x": 4, "y": 4, "z": 8}
TURNS = (0, 0, 1, 2, 0, 0, 1, 2, 1, 2, 0, 0, 0, 1, 2, 0, 1, 2)
WORK = (2, 3, 2, 0, 1, 3, 2, 0, 4, 0, 6, 17, 0, 0, 0, 0, 0, 0)


def plan(order):
    ring = [(d, s) for d in order for s in range(SIZE[d] // 2)]
    return [("z", None)] + ring[SIZE["z"] // 2 :] if order[0] == "z" else ring


def copies_count():
    total = 0
    for _, _, order in PARTS:
        total += sum(SIZE["z"] - 1 if s is None else 2 for _, s in plan(order)) + 1 + SIZE[order[2]]
    return total


class Spread:
    def __init__(self, own, out, send, recv, local):
        r = lax.axis_index("rows")
        self.me = {"x": r // 8, "y": (r // 2) % 4, "z": lax.axis_index("hst")}
        self.c = r % 2
        self.own, self.out, self.send, self.recv = own, out, send, recv
        self.used = 0
        self.started, self.given = [], []
        self.step = [0] * len(PARTS)
        self.pending = [None] * len(PARTS)
        me = self.me
        self.local = pltpu.make_async_copy(
            own,
            out.at[pl.ds(me["x"], 1), pl.ds(me["y"], 1), pl.ds(self.c, 1), pl.ds(me["z"], 1)],
            local,
        )

    def device(self, d=None, by=0, core=None):
        at = dict(self.me)
        if d is not None:
            at[d] = (at[d] + by + SIZE[d]) % SIZE[d]
        c = self.c if core is None else core
        return ((at["x"] * 4 + at["y"]) * 2 + c, at["z"])

    def region(self, part, d, by, half=None):
        first, count, order = PARTS[part]
        full = order[: order.index(d)]
        index = {}
        for e in "xyz":
            if e == d:
                index[e] = pl.ds((self.me[e] + by + SIZE[e]) % SIZE[e], 1)
            elif e in full:
                index[e] = pl.ds(0, SIZE[e])
            else:
                index[e] = pl.ds(self.me[e], 1)
        if half is not None:
            if full:
                n = SIZE[full[0]] // 2
                index[full[0]] = pl.ds(half * n, n)
            else:
                cut = (count + 31) // 32 * 16
                first, count = (first, cut) if half == 0 else (first + cut, count - cut)
        return self.out.at[
            index["x"], index["y"], pl.ds(self.c, 1), index["z"], pl.ds(first, count), :
        ]

    def copy(self, ref, to, src=None):
        i = self.used
        self.used += 1
        c = pltpu.make_async_remote_copy(
            src_ref=ref if src is None else src,
            dst_ref=ref,
            send_sem=self.send.at[i],
            recv_sem=self.recv.at[i],
            device_id=to,
            device_id_type=MESH,
        )
        c.start()
        self.started.append(c)
        return c

    def start(self, part, step, way):
        first, count, order = PARTS[part]
        d, s = plan(order)[step]
        src = self.own.at[:, :, :, :, pl.ds(first, count), :] if step == 0 else None
        if s is None:
            return self.copy(self.region(part, d, 0), self.device(d, way), src), -way, None
        half = None if s < SIZE[d] // 2 - 1 else (0 if way == 1 else 1)
        ref = self.region(part, d, -way * s, half)
        return self.copy(ref, self.device(d, way), src), -way * (s + 1), half

    def ways(self, part):
        _, s = plan(PARTS[part][2])[self.step[part]]
        return range(1, SIZE["z"]) if s is None else (1, -1)

    def first(self):
        for part in range(len(PARTS)):
            self.pending[part] = [self.start(part, 0, way) for way in self.ways(part)]

    def give(self, ref):
        self.given.append(self.copy(ref, self.device(core=1 - self.c)))

    def turn(self, part):
        order = PARTS[part][2]
        steps = plan(order)
        step = self.step[part]
        d, s = steps[step]
        more = step + 1 < len(steps)
        same = more and steps[step + 1][0] == d
        arrived, self.pending[part] = self.pending[part], []
        self.step[part] += 1
        for i, (copy, _, _) in enumerate(arrived):
            copy.wait_recv()
            if same:
                self.pending[part].append(self.start(part, step + 1, (1, -1)[i]))
        if more and not same:
            self.pending[part] = [self.start(part, step + 1, way) for way in self.ways(part)]
            if steps[step + 1][0] == order[2]:
                self.give(self.region(part, order[2], 0))
        if d == order[2]:
            for _, by, half in arrived:
                self.give(self.region(part, d, by, half))

    def finish(self):
        for c in self.given:
            c.wait_recv()
        for c in self.started:
            c.wait_send()


ROWS, HST = 32, 8
PEERS = HST - 1 + ROWS - 1


def greet_all():
    r, z = lax.axis_index("rows"), lax.axis_index("hst")
    barrier = pltpu.get_barrier_semaphore()
    for k in range(1, HST):
        pl.semaphore_signal(barrier, inc=1, device_id=(r, (z + k) % HST), device_id_type=MESH)

    def tell(k, carry):
        pl.semaphore_signal(barrier, inc=1, device_id=((r + k) % ROWS, z), device_id_type=MESH)
        return carry

    lax.fori_loop(1, ROWS, tell, 0)
    pl.semaphore_wait(barrier, PEERS)


class Exchange:
    def __init__(self, src, mid, dst, send, recv):
        self.r, self.z = lax.axis_index("rows"), lax.axis_index("hst")
        self.src, self.mid, self.dst, self.send, self.recv = src, mid, dst, send, recv

    def down(self, k):
        return pltpu.make_async_remote_copy(
            src_ref=self.src.at[:, pl.ds((self.z + k) % HST, 1)],
            dst_ref=self.mid.at[:, pl.ds(self.z, 1)],
            send_sem=self.send.at[k - 1],
            recv_sem=self.recv.at[k - 1],
            device_id=(self.r, (self.z + k) % HST),
            device_id_type=MESH,
        )

    def across(self, k):
        to = (self.r + k) % ROWS
        return pltpu.make_async_remote_copy(
            src_ref=self.mid.at[pl.ds(to, 1)],
            dst_ref=self.dst.at[pl.ds(self.r, 1)],
            send_sem=self.send.at[HST - 2 + k],
            recv_sem=self.recv.at[HST - 2 + k],
            device_id=(to, self.z),
            device_id_type=MESH,
        )

    def each(self, first, last, act):
        def body(k, carry):
            act(k)
            return carry

        lax.fori_loop(first, last, body, 0)

    def begin(self):
        self.each(1, HST, lambda k: self.down(k).start())
        self.mid[:, pl.ds(self.z, 1)] = self.src[:, pl.ds(self.z, 1)]

    def turn(self):
        self.each(1, HST, lambda k: self.down(k).wait_recv())
        self.each(1, ROWS, lambda k: self.across(k).start())
        self.dst[pl.ds(self.r, 1)] = self.mid[pl.ds(self.r, 1)]

    def finish(self):
        self.each(1, ROWS, lambda k: self.across(k).wait_recv())
        self.each(1, HST, lambda k: self.down(k).wait_send())
        self.each(1, ROWS, lambda k: self.across(k).wait_send())


def route_kernel(
    own_ref, slot_ref, bag_ref, w_ref, block_ref,
    got_ref, rank_ref, everyone_ref,
    acc, base, upper, meta_ref, mid_ref, send, recv, placed, meta_send, meta_recv,
):
    greet_all()
    spread = Spread(block_ref, everyone_ref, send, recv, placed)
    spread.local.start()
    spread.first()
    steps, k = own_ref.shape
    n = acc.shape[0]
    acc[...] = jnp.zeros_like(acc)
    base[...] = jnp.zeros_like(base)
    upper[...] = onehot(iota((k, k), 0) < iota((k, k), 1))

    def step(i, carry):
        row = pl.ds(i, 1)
        mask = iota((n, k), 0) == own_ref[row, :]
        a = onehot(mask)
        before = jnp.dot(a, upper[...], preferred_element_type=F32)
        start = jnp.concatenate([base[...]] * (k // RP), axis=1)
        rank = jnp.sum(jnp.where(mask, before + start, 0.0), axis=0, keepdims=True)
        base[...] += jnp.dot(a, jnp.ones((k, RP), BF), preferred_element_type=F32)
        rank = rank.astype(I32)
        rank_ref[row, :] = rank
        put = iota((RP, k), 0) == rank
        slot = slot_ref[row, :]
        parts = [
            (slot >> 8).astype(F32),
            (slot & 255).astype(F32),
            bag_ref[row, :].astype(F32),
            w_ref[row, :],
        ]
        b = jnp.concatenate([jnp.where(put, p, 0.0).astype(BF) for p in parts], axis=0)
        acc[...] += lax.dot_general(a, b, (((1,), (1,)), ((), ())), preferred_element_type=F32)
        return carry

    exchange = Exchange(meta_ref, mid_ref, got_ref, meta_send, meta_recv)
    done = 0
    for i, (part, work) in enumerate(zip(TURNS, WORK)):
        if work:
            upto = steps if i == 11 else done + work
            lax.fori_loop(done, upto, step, 0)
            done = upto
        if i == 0:
            spread.local.wait()
        if i == 12:
            slots = (acc[:, 0:RP] * 256.0 + acc[:, RP : 2 * RP]).astype(I32)
            ids = slots * FIELD + acc[:, 2 * RP : 3 * RP].astype(I32)
            meta_ref[:, :, 0, :] = ids.reshape(ROWS, HST, RP)
            codes = (acc[:, 3 * RP : 4 * RP] * float(FIELD)).astype(I32)
            meta_ref[:, :, 1, :] = codes.reshape(ROWS, HST, RP)
            exchange.begin()
        if i == 13:
            exchange.turn()
        spread.turn(part)
    exchange.finish()
    spread.finish()


def spots(slot, k):
    hi = jnp.broadcast_to((slot >> 4).astype(F32), (16, k)).astype(BF)
    lo = jnp.broadcast_to((slot & 15).astype(F32), (16, k)).astype(BF)
    return hi, lo == iota((16, k), 0).astype(F32).astype(BF)


def tile_of(hi, base, first, count):
    zero = jnp.zeros_like(base)
    return jnp.concatenate(
        [jnp.where(hi == jnp.asarray(first + t, BF), base, zero) for t in range(count)], axis=0
    )


def owner_kernel(
    live_ref, count_ref, id_ref, w_ref, g_ref, table_ref, states_ref,
    prod_ref, new_table_ref, new_states_ref, tab, grad, hot,
):
    c = pl.program_id(0)
    touched, width = table_ref.shape
    k = id_ref.shape[2]
    bags = g_ref.shape[2]
    blocks = touched // 128

    @pl.when(c == 0)
    def _():
        grad[...] = jnp.zeros_like(grad)
        for m in range(blocks):
            t = table_ref[m * 128 : (m + 1) * 128, :].T
            high = t.astype(BF)
            tab[0:width, m * 128 : (m + 1) * 128] = high
            tab[width : 2 * width, m * 128 : (m + 1) * 128] = (t - high.astype(F32)).astype(BF)

    prod_ref[...] = jnp.zeros_like(prod_ref)

    def row_of(ref, q, rows):
        return jnp.concatenate([ref[0, pl.ds(q + i, 1), :] for i in range(rows)], axis=1)

    def take(q, first, count, rows):
        wide = rows * k
        here = hot.at[:, 0:wide]
        hi, at = spots(row_of(id_ref, q, rows) >> 16, wide)
        w = row_of(w_ref, q, rows).astype(F32) * (1.0 / FIELD)
        w = jnp.broadcast_to(w, (16, wide)).astype(BF)
        base = jnp.where(at, w, jnp.zeros_like(w))
        for m in range(touched // 256):
            here[m * 256 : (m + 1) * 256, :] = tile_of(hi, base, 16 * m, 16)
        rows_at = jnp.dot(tab[...], here[...], preferred_element_type=F32)
        parts = []
        for i in range(rows):
            per = k // count
            bag = id_ref[0, pl.ds(q + i, 1), :] & (FIELD - 1)
            bag = bag + lax.broadcasted_iota(I32, (1, k), 1) // per * bags
            hi, at = spots(bag, k)
            one = jnp.where(at, jnp.ones((16, k), BF), jnp.zeros((16, k), BF))
            got = jnp.zeros((width, k), F32)
            for s in range(count):
                pick = tile_of(hi, one, bags // 16 * s, bags // 16)
                got += jnp.dot(g_ref[first + i * count + s], pick, preferred_element_type=F32)
            parts.append(got)
        got = jnp.concatenate(parts, axis=1)
        dots = jnp.sum((rows_at[0:width] + rows_at[width:]) * got, axis=0, keepdims=True)
        for i in range(rows):
            prod_ref[0, pl.ds(q + i, 1), :] = dots[:, i * k : (i + 1) * k]
        got = got.astype(BF)
        for m in range(touched // 256):
            at = slice(m * 256, (m + 1) * 256)
            grad[:, at] += lax.dot_general(
                got, here[at, :], (((1,), (1,)), ((), ())), preferred_element_type=F32
            )

    def low(i, carry):
        q = i * 2

        @pl.when(live_ref[c * 8 + q] + live_ref[c * 8 + q + 1] != 0)
        def _():
            take(q, q * 4, 4, 2)

        return carry

    def high_ranks(q, carry):
        @pl.when(live_ref[c * 8 + q] != 0)
        def _():
            take(q, 0, 16, 1)

        return carry

    lax.fori_loop(0, 2, low, 0)
    lax.fori_loop(4, 6, high_ranks, 0)

    @pl.when(c == pl.num_programs(0) - 1)
    def _():
        for m in range(blocks):
            at = slice(m * 128, (m + 1) * 128)
            r = grad[:, at]
            summed = states_ref[m : m + 1, :] + jnp.mean(r * r, axis=0, keepdims=True)
            delta = learn_rate * r / (jnp.sqrt(summed) + epsilon_value)
            left = count_ref[0] - m * 128
            updated = table_ref[at, :] - delta.T
            new_table_ref[at, :] = jnp.where(iota((128, width), 0) < left, updated, 0.0)
            new_states_ref[m : m + 1, :] = jnp.where(iota((1, 128), 1) < left, summed, 0.0)


def back_kernel(own_ref, rank_ref, w_ref, prod_ref, out_ref, parts):
    steps, k = own_ref.shape
    n = prod_ref.shape[0]
    t = prod_ref[...].T
    high = t.astype(BF)
    parts[0:RP, :] = high
    parts[RP : 2 * RP, :] = (t - high.astype(F32)).astype(BF)
    unroll = 4

    def step(i, carry):
        for j in range(unroll):
            row = pl.ds(i * unroll + j, 1)
            hi, at = spots(own_ref[row, :], k)
            one = jnp.where(at, jnp.ones((16, k), BF), jnp.zeros((16, k), BF))
            x = jnp.dot(parts[...], tile_of(hi, one, 0, n // 16), preferred_element_type=F32)
            x = jnp.where(iota((RP, k), 0) == rank_ref[row, :], x[0:RP] + x[RP:], 0.0)
            out_ref[row, :] = jnp.sum(x, axis=0, keepdims=True) / w_ref[row, :]
        return carry

    lax.fori_loop(0, steps // unroll, step, 0)


def local(grad_pooled, weights, owner, slot, lengths, counts, table, states):
    devices = lax.axis_size("rows") * lax.axis_size("hst")
    bags, features, per_bag = weights.shape
    width = grad_pooled.shape[2]
    touched = table.shape[0]
    total_ids = bags * features * per_bag
    n_bags = bags * features
    k1 = 256
    steps = total_ids // k1
    vmem = pl.BlockSpec(memory_space=pltpu.VMEM)
    live = jnp.arange(per_bag, dtype=I32)[None, None, :] < lengths[:, :, None]
    own = jnp.where(live, owner, -1).reshape(steps, k1)
    slots = slot.reshape(steps, k1)
    w = weights.astype(F32).reshape(steps, k1)
    bag = jnp.asarray((np.arange(total_ids) // per_bag).reshape(steps, k1), I32)
    g = grad_pooled.reshape(n_bags, width)

    flights = copies_count()
    got_meta, rank, everyone = pl.pallas_call(
        route_kernel,
        out_shape=(
            jax.ShapeDtypeStruct((ROWS, HST, 2, RP), I32),
            jax.ShapeDtypeStruct((steps, k1), I32),
            jax.ShapeDtypeStruct((4, 4, 2, 8, width, n_bags), BF),
        ),
        in_specs=[vmem] * 5,
        out_specs=(vmem, vmem, pl.BlockSpec(memory_space=pl.ANY)),
        scratch_shapes=[
            pltpu.VMEM((devices, 4 * RP), F32),
            pltpu.VMEM((devices, RP), F32),
            pltpu.VMEM((k1, k1), BF),
            pltpu.VMEM((ROWS, HST, 2, RP), I32),
            pltpu.VMEM((ROWS, HST, 2, RP), I32),
            pltpu.SemaphoreType.DMA((flights,)),
            pltpu.SemaphoreType.DMA((flights,)),
            pltpu.SemaphoreType.DMA,
            pltpu.SemaphoreType.DMA((PEERS,)),
            pltpu.SemaphoreType.DMA((PEERS,)),
        ],
        compiler_params=pltpu.CompilerParams(collective_id=0, has_side_effects=True),
        name="route",
    )(own, slots, bag, w, g.T.reshape(1, 1, 1, 1, width, n_bags))
    everyone = everyone.reshape(devices, width, n_bags)
    got_meta = got_meta.reshape(devices, 2, RP)

    srcs = 16
    groups = devices // srcs
    k2 = 256

    def in_rows(v):
        return jnp.concatenate(
            [
                v[:, 0:64].reshape(groups, 4, k2),
                v[:, 64:80].reshape(groups, 1, k2),
                v[:, 80:96].reshape(groups, 1, k2),
                jnp.zeros((groups, 2, k2), v.dtype),
            ],
            axis=1,
        )

    got_ids = in_rows(got_meta[:, 0, :])
    got_w = in_rows(got_meta[:, 1, :])
    active = (jnp.max(got_w, axis=2) > 0).astype(I32).reshape(-1)

    prods, new_table, new_states = pl.pallas_call(
        owner_kernel,
        grid_spec=pltpu.PrefetchScalarGridSpec(
            num_scalar_prefetch=2,
            grid=(groups,),
            in_specs=[
                pl.BlockSpec((1, 8, k2), lambda c, *_: (c, 0, 0)),
                pl.BlockSpec((1, 8, k2), lambda c, *_: (c, 0, 0)),
                pl.BlockSpec((srcs, width, n_bags), lambda c, *_: (c, 0, 0)),
                pl.BlockSpec((touched, width), lambda c, *_: (0, 0)),
                pl.BlockSpec((touched // 128, 128), lambda c, *_: (0, 0)),
            ],
            out_specs=(
                pl.BlockSpec((1, 8, k2), lambda c, *_: (c, 0, 0)),
                pl.BlockSpec((touched, width), lambda c, *_: (0, 0)),
                pl.BlockSpec((touched // 128, 128), lambda c, *_: (0, 0)),
            ),
            scratch_shapes=[
                pltpu.VMEM((2 * width, touched), BF),
                pltpu.VMEM((width, touched), F32),
                pltpu.VMEM((touched, 2 * k2), BF),
            ],
        ),
        out_shape=(
            jax.ShapeDtypeStruct((groups, 8, k2), F32),
            jax.ShapeDtypeStruct((touched, width), F32),
            jax.ShapeDtypeStruct((touched // 128, 128), F32),
        ),
        compiler_params=params("arbitrary"),
        name="owner_step",
    )(active, counts, got_ids, got_w, everyone, table, states.reshape(touched // 128, 128))

    back = jnp.concatenate(
        [
            prods[:, 0:4].reshape(devices, 64),
            prods[:, 4].reshape(devices, 16),
            prods[:, 5].reshape(devices, 16),
        ],
        axis=1,
    )
    back = jnp.pad(back, ((0, 0), (0, RP - CAP)))
    returned = lax.all_to_all(back, BOTH, split_axis=0, concat_axis=0, tiled=True)
    weight_grad = pl.pallas_call(
        back_kernel,
        out_shape=jax.ShapeDtypeStruct((steps, k1), F32),
        in_specs=[vmem] * 4,
        out_specs=vmem,
        scratch_shapes=[pltpu.VMEM((2 * RP, devices), BF)],
        name="back",
    )(own, rank, w, returned)
    return (weight_grad.reshape(weights.shape), new_table, new_states.reshape(-1))


def solution(mesh):
    return jax.shard_map(
        local,
        mesh=mesh,
        in_specs=(
            P(BOTH, None, None),
            P(BOTH, None, None),
            P(BOTH, None, None),
            P(BOTH, None, None),
            P(BOTH, None),
            P(BOTH),
            P(BOTH, None),
            P(BOTH),
        ),
        out_specs=(P(BOTH, None, None), P(BOTH, None), P(BOTH)),
        check_vma=False,
    )
```

```python
import functools
import jax
import jax.numpy as jnp
import numpy as np
from jax import lax
from jax.experimental import pallas as pl
from jax.experimental.pallas import tpu as pltpu
from jax.sharding import PartitionSpec as P

learn_rate = 0.1
epsilon_value = 1e-08
CAP = 96
RP = 128
FIELD = 65536
SLOT_BITS = 11
BOTH = ("rows", "hst")
BF = jnp.bfloat16
F32 = jnp.float32
I32 = jnp.int32


def onehot(mask):
    return jnp.where(mask, 1.0, 0.0).astype(BF)


def iota(shape, dim):
    return lax.broadcasted_iota(I32, shape, dim)


def params(*sem):
    return pltpu.CompilerParams(dimension_semantics=sem or None)


MESH = pl.DeviceIdType.MESH
PARTS = ((0, 32, "xyz"), (32, 48, "zyx"), (80, 48, "zxy"))
SIZE = {"x": 4, "y": 4, "z": 8}
TURNS = (0, 0, 1, 2, 0, 0, 1, 2, 1, 2, 0, 0, 0, 1, 2, 0, 1, 2)
WORK = (2, 3, 2, 0, 1, 3, 2, 0, 4, 0, 6, 17, 0, 0, 0, 0, 0, 0)


def plan(order):
    ring = [(d, s) for d in order for s in range(SIZE[d] // 2)]
    return [("z", None)] + ring[SIZE["z"] // 2 :] if order[0] == "z" else ring


def copies_count():
    total = 0
    for _, _, order in PARTS:
        total += sum(SIZE["z"] - 1 if s is None else 2 for _, s in plan(order)) + 1 + SIZE[order[2]]
    return total


class Spread:
    def __init__(self, own, out, send, recv, local):
        r = lax.axis_index("rows")
        self.me = {"x": r // 8, "y": (r // 2) % 4, "z": lax.axis_index("hst")}
        self.c = r % 2
        self.own, self.out, self.send, self.recv = own, out, send, recv
        self.used = 0
        self.started, self.given = [], []
        self.step = [0] * len(PARTS)
        self.pending = [None] * len(PARTS)
        me = self.me
        self.local = pltpu.make_async_copy(
            own,
            out.at[pl.ds(me["x"], 1), pl.ds(me["y"], 1), pl.ds(self.c, 1), pl.ds(me["z"], 1)],
            local,
        )

    def device(self, d=None, by=0, core=None):
        at = dict(self.me)
        if d is not None:
            at[d] = (at[d] + by + SIZE[d]) % SIZE[d]
        c = self.c if core is None else core
        return ((at["x"] * 4 + at["y"]) * 2 + c, at["z"])

    def region(self, part, d, by, half=None):
        first, count, order = PARTS[part]
        full = order[: order.index(d)]
        index = {}
        for e in "xyz":
            if e == d:
                index[e] = pl.ds((self.me[e] + by + SIZE[e]) % SIZE[e], 1)
            elif e in full:
                index[e] = pl.ds(0, SIZE[e])
            else:
                index[e] = pl.ds(self.me[e], 1)
        if half is not None:
            if full:
                n = SIZE[full[0]] // 2
                index[full[0]] = pl.ds(half * n, n)
            else:
                cut = (count + 31) // 32 * 16
                first, count = (first, cut) if half == 0 else (first + cut, count - cut)
        return self.out.at[
            index["x"], index["y"], pl.ds(self.c, 1), index["z"], pl.ds(first, count), :
        ]

    def copy(self, ref, to, src=None):
        i = self.used
        self.used += 1
        c = pltpu.make_async_remote_copy(
            src_ref=ref if src is None else src,
            dst_ref=ref,
            send_sem=self.send.at[i],
            recv_sem=self.recv.at[i],
            device_id=to,
            device_id_type=MESH,
        )
        c.start()
        self.started.append(c)
        return c

    def start(self, part, step, way):
        first, count, order = PARTS[part]
        d, s = plan(order)[step]
        src = self.own.at[:, :, :, :, pl.ds(first, count), :] if step == 0 else None
        if s is None:
            return self.copy(self.region(part, d, 0), self.device(d, way), src), -way, None
        half = None if s < SIZE[d] // 2 - 1 else (0 if way == 1 else 1)
        ref = self.region(part, d, -way * s, half)
        return self.copy(ref, self.device(d, way), src), -way * (s + 1), half

    def ways(self, part):
        _, s = plan(PARTS[part][2])[self.step[part]]
        return range(1, SIZE["z"]) if s is None else (1, -1)

    def first(self):
        for part in range(len(PARTS)):
            self.pending[part] = [self.start(part, 0, way) for way in self.ways(part)]

    def give(self, ref):
        self.given.append(self.copy(ref, self.device(core=1 - self.c)))

    def turn(self, part):
        order = PARTS[part][2]
        steps = plan(order)
        step = self.step[part]
        d, s = steps[step]
        more = step + 1 < len(steps)
        same = more and steps[step + 1][0] == d
        arrived, self.pending[part] = self.pending[part], []
        self.step[part] += 1
        for i, (copy, _, _) in enumerate(arrived):
            copy.wait_recv()
            if same:
                self.pending[part].append(self.start(part, step + 1, (1, -1)[i]))
        if more and not same:
            self.pending[part] = [self.start(part, step + 1, way) for way in self.ways(part)]
            if steps[step + 1][0] == order[2]:
                self.give(self.region(part, order[2], 0))
        if d == order[2]:
            for _, by, half in arrived:
                self.give(self.region(part, d, by, half))

    def finish(self):
        for c in self.given:
            c.wait_recv()
        for c in self.started:
            c.wait_send()


ROWS, HST = 32, 8
PEERS = HST - 1 + ROWS - 1


def greet_all():
    r, z = lax.axis_index("rows"), lax.axis_index("hst")
    barrier = pltpu.get_barrier_semaphore()
    for k in range(1, HST):
        pl.semaphore_signal(barrier, inc=1, device_id=(r, (z + k) % HST), device_id_type=MESH)

    def tell(k, carry):
        pl.semaphore_signal(barrier, inc=1, device_id=((r + k) % ROWS, z), device_id_type=MESH)
        return carry

    lax.fori_loop(1, ROWS, tell, 0)
    pl.semaphore_wait(barrier, PEERS)


class Exchange:
    def __init__(self, src, mid, dst, send, recv):
        self.r, self.z = lax.axis_index("rows"), lax.axis_index("hst")
        self.src, self.mid, self.dst, self.send, self.recv = src, mid, dst, send, recv

    def down(self, k):
        return pltpu.make_async_remote_copy(
            src_ref=self.src.at[:, pl.ds((self.z + k) % HST, 1)],
            dst_ref=self.mid.at[:, pl.ds(self.z, 1)],
            send_sem=self.send.at[k - 1],
            recv_sem=self.recv.at[k - 1],
            device_id=(self.r, (self.z + k) % HST),
            device_id_type=MESH,
        )

    def across(self, k):
        to = (self.r + k) % ROWS
        return pltpu.make_async_remote_copy(
            src_ref=self.mid.at[pl.ds(to, 1)],
            dst_ref=self.dst.at[pl.ds(self.r, 1)],
            send_sem=self.send.at[HST - 2 + k],
            recv_sem=self.recv.at[HST - 2 + k],
            device_id=(to, self.z),
            device_id_type=MESH,
        )

    def each(self, first, last, act):
        def body(k, carry):
            act(k)
            return carry

        lax.fori_loop(first, last, body, 0)

    def begin(self):
        self.each(1, HST, lambda k: self.down(k).start())
        self.mid[:, pl.ds(self.z, 1)] = self.src[:, pl.ds(self.z, 1)]

    def turn(self):
        self.each(1, HST, lambda k: self.down(k).wait_recv())
        self.each(1, ROWS, lambda k: self.across(k).start())
        self.dst[pl.ds(self.r, 1)] = self.mid[pl.ds(self.r, 1)]

    def finish(self):
        self.each(1, ROWS, lambda k: self.across(k).wait_recv())
        self.each(1, HST, lambda k: self.down(k).wait_send())
        self.each(1, ROWS, lambda k: self.across(k).wait_send())


def route_kernel(
    key_ref, bag_ref, w_ref, block_ref,
    got_ref, rank_ref, everyone_ref,
    acc, base, upper, meta_ref, mid_ref, send, recv, placed, meta_send, meta_recv,
):
    greet_all()
    spread = Spread(block_ref, everyone_ref, send, recv, placed)
    spread.local.start()
    spread.first()
    steps, k = key_ref.shape
    n = acc.shape[0]
    acc[...] = jnp.zeros_like(acc)
    base[...] = jnp.zeros_like(base)
    upper[...] = onehot(iota((k, k), 0) < iota((k, k), 1))

    def step(i, carry):
        row = pl.ds(i, 1)
        key = key_ref[row, :]
        mask = iota((n, k), 0) == (key >> SLOT_BITS)
        a = onehot(mask)
        before = jnp.dot(a, upper[...], preferred_element_type=F32)
        start = jnp.concatenate([base[...]] * (k // RP), axis=1)
        rank = jnp.sum(jnp.where(mask, before + start, 0.0), axis=0, keepdims=True)
        base[...] += jnp.dot(a, jnp.ones((k, RP), BF), preferred_element_type=F32)
        rank = rank.astype(I32)
        rank_ref[row, :] = rank
        put = iota((RP, k), 0) == rank
        slot = key & ((1 << SLOT_BITS) - 1)
        parts = [
            (slot >> 8).astype(F32),
            (slot & 255).astype(F32),
            bag_ref[row, :].astype(F32),
            w_ref[row, :],
        ]
        b = jnp.concatenate([jnp.where(put, p, 0.0).astype(BF) for p in parts], axis=0)
        acc[...] += lax.dot_general(a, b, (((1,), (1,)), ((), ())), preferred_element_type=F32)
        return carry

    exchange = Exchange(meta_ref, mid_ref, got_ref, meta_send, meta_recv)
    done = 0
    for i, (part, work) in enumerate(zip(TURNS, WORK)):
        if work:
            upto = steps if i == 11 else done + work
            lax.fori_loop(done, upto, step, 0)
            done = upto
        if i == 0:
            spread.local.wait()
        if i == 12:
            slots = (acc[:, 0:RP] * 256.0 + acc[:, RP : 2 * RP]).astype(I32)
            ids = slots * FIELD + acc[:, 2 * RP : 3 * RP].astype(I32)
            meta_ref[:, :, 0, :] = ids.reshape(ROWS, HST, RP)
            codes = (acc[:, 3 * RP : 4 * RP] * float(FIELD)).astype(I32)
            meta_ref[:, :, 1, :] = codes.reshape(ROWS, HST, RP)
            exchange.begin()
        if i == 15:
            exchange.turn()
        spread.turn(part)
    exchange.finish()
    spread.finish()


def spots(slot, k):
    hi = jnp.broadcast_to((slot >> 4).astype(F32), (16, k)).astype(BF)
    lo = jnp.broadcast_to((slot & 15).astype(F32), (16, k)).astype(BF)
    return hi, lo == iota((16, k), 0).astype(F32).astype(BF)


def tile_of(hi, base, first, count):
    zero = jnp.zeros_like(base)
    return jnp.concatenate(
        [jnp.where(hi == jnp.asarray(first + t, BF), base, zero) for t in range(count)], axis=0
    )


def owner_kernel(
    live_ref, count_ref, id_ref, w_ref, g_ref, table_ref, states_ref,
    prod_ref, new_table_ref, new_states_ref, tab, grad, hot,
):
    c = pl.program_id(0)
    touched, width = table_ref.shape
    k = id_ref.shape[2]
    bags = g_ref.shape[2]
    blocks = touched // 128

    @pl.when(c == 0)
    def _():
        grad[...] = jnp.zeros_like(grad)
        for m in range(blocks):
            t = table_ref[m * 128 : (m + 1) * 128, :].T
            high = t.astype(BF)
            tab[0:width, m * 128 : (m + 1) * 128] = high
            tab[width : 2 * width, m * 128 : (m + 1) * 128] = (t - high.astype(F32)).astype(BF)

    prod_ref[...] = jnp.zeros_like(prod_ref)

    def row_of(ref, q, rows):
        return jnp.concatenate([ref[0, pl.ds(q + i, 1), :] for i in range(rows)], axis=1)

    def take(q, first, count, rows):
        wide = rows * k
        here = hot.at[:, 0:wide]
        hi, at = spots(row_of(id_ref, q, rows) >> 16, wide)
        w = row_of(w_ref, q, rows).astype(F32) * (1.0 / FIELD)
        w = jnp.broadcast_to(w, (16, wide)).astype(BF)
        base = jnp.where(at, w, jnp.zeros_like(w))
        for m in range(touched // 256):
            here[m * 256 : (m + 1) * 256, :] = tile_of(hi, base, 16 * m, 16)
        rows_at = jnp.dot(tab[...], here[...], preferred_element_type=F32)
        parts = []
        for i in range(rows):
            per = k // count
            bag = id_ref[0, pl.ds(q + i, 1), :] & (FIELD - 1)
            bag = bag + lax.broadcasted_iota(I32, (1, k), 1) // per * bags
            hi, at = spots(bag, k)
            one = jnp.where(at, jnp.ones((16, k), BF), jnp.zeros((16, k), BF))
            got = jnp.zeros((width, k), F32)
            for s in range(count):
                pick = tile_of(hi, one, bags // 16 * s, bags // 16)
                got += jnp.dot(g_ref[first + i * count + s], pick, preferred_element_type=F32)
            parts.append(got)
        got = jnp.concatenate(parts, axis=1)
        dots = jnp.sum((rows_at[0:width] + rows_at[width:]) * got, axis=0, keepdims=True)
        for i in range(rows):
            prod_ref[0, pl.ds(q + i, 1), :] = dots[:, i * k : (i + 1) * k]
        got = got.astype(BF)
        for m in range(touched // 256):
            at = slice(m * 256, (m + 1) * 256)
            grad[:, at] += lax.dot_general(
                got, here[at, :], (((1,), (1,)), ((), ())), preferred_element_type=F32
            )

    def low(i, carry):
        q = i * 2

        @pl.when(live_ref[c * 8 + q] + live_ref[c * 8 + q + 1] != 0)
        def _():
            take(q, q * 4, 4, 2)

        return carry

    def high_ranks(q, carry):
        @pl.when(live_ref[c * 8 + q] != 0)
        def _():
            take(q, 0, 16, 1)

        return carry

    lax.fori_loop(0, 2, low, 0)
    lax.fori_loop(4, 6, high_ranks, 0)

    @pl.when(c == pl.num_programs(0) - 1)
    def _():
        for m in range(blocks):
            at = slice(m * 128, (m + 1) * 128)
            r = grad[:, at]
            summed = states_ref[m : m + 1, :] + jnp.mean(r * r, axis=0, keepdims=True)
            delta = learn_rate * r / (jnp.sqrt(summed) + epsilon_value)
            left = count_ref[0] - m * 128
            updated = table_ref[at, :] - delta.T
            new_table_ref[at, :] = jnp.where(iota((128, width), 0) < left, updated, 0.0)
            new_states_ref[m : m + 1, :] = jnp.where(iota((1, 128), 1) < left, summed, 0.0)


def back_kernel(key_ref, rank_ref, w_ref, prod_ref, out_ref, parts):
    steps, k = key_ref.shape
    n = prod_ref.shape[0]
    t = prod_ref[...].T
    high = t.astype(BF)
    parts[0:RP, :] = high
    parts[RP : 2 * RP, :] = (t - high.astype(F32)).astype(BF)
    unroll = 4

    def step(i, carry):
        for j in range(unroll):
            row = pl.ds(i * unroll + j, 1)
            hi, at = spots(key_ref[row, :] >> SLOT_BITS, k)
            one = jnp.where(at, jnp.ones((16, k), BF), jnp.zeros((16, k), BF))
            x = jnp.dot(parts[...], tile_of(hi, one, 0, n // 16), preferred_element_type=F32)
            x = jnp.where(iota((RP, k), 0) == rank_ref[row, :], x[0:RP] + x[RP:], 0.0)
            out_ref[row, :] = jnp.sum(x, axis=0, keepdims=True) / w_ref[row, :]
        return carry

    lax.fori_loop(0, steps // unroll, step, 0)


def local(grad_pooled, weights, owner, slot, lengths, counts, table, states):
    devices = lax.axis_size("rows") * lax.axis_size("hst")
    bags, features, per_bag = weights.shape
    width = grad_pooled.shape[2]
    touched = table.shape[0]
    total_ids = bags * features * per_bag
    n_bags = bags * features
    k1 = 256
    steps = total_ids // k1
    vmem = pl.BlockSpec(memory_space=pltpu.VMEM)
    live = jnp.arange(per_bag, dtype=I32)[None, None, :] < lengths[:, :, None]
    assert touched == 1 << SLOT_BITS
    key = jnp.where(live, owner * touched + slot, -1).reshape(steps, k1)
    w = weights.astype(F32).reshape(steps, k1)
    bag = jnp.asarray((np.arange(total_ids) // per_bag).reshape(steps, k1), I32)
    g = grad_pooled.reshape(n_bags, width)

    flights = copies_count()
    got_meta, rank, everyone = pl.pallas_call(
        route_kernel,
        out_shape=(
            jax.ShapeDtypeStruct((ROWS, HST, 2, RP), I32),
            jax.ShapeDtypeStruct((steps, k1), I32),
            jax.ShapeDtypeStruct((4, 4, 2, 8, width, n_bags), BF),
        ),
        in_specs=[vmem] * 4,
        out_specs=(vmem, vmem, pl.BlockSpec(memory_space=pl.ANY)),
        scratch_shapes=[
            pltpu.VMEM((devices, 4 * RP), F32),
            pltpu.VMEM((devices, RP), F32),
            pltpu.VMEM((k1, k1), BF),
            pltpu.VMEM((ROWS, HST, 2, RP), I32),
            pltpu.VMEM((ROWS, HST, 2, RP), I32),
            pltpu.SemaphoreType.DMA((flights,)),
            pltpu.SemaphoreType.DMA((flights,)),
            pltpu.SemaphoreType.DMA,
            pltpu.SemaphoreType.DMA((PEERS,)),
            pltpu.SemaphoreType.DMA((PEERS,)),
        ],
        compiler_params=pltpu.CompilerParams(collective_id=0, has_side_effects=True),
        name="route",
    )(key, bag, w, g.T.reshape(1, 1, 1, 1, width, n_bags))
    everyone = everyone.reshape(devices, width, n_bags)
    got_meta = got_meta.reshape(devices, 2, RP)

    srcs = 16
    groups = devices // srcs
    k2 = 256

    def in_rows(v):
        return jnp.concatenate(
            [
                v[:, 0:64].reshape(groups, 4, k2),
                v[:, 64:80].reshape(groups, 1, k2),
                v[:, 80:96].reshape(groups, 1, k2),
                jnp.zeros((groups, 2, k2), v.dtype),
            ],
            axis=1,
        )

    got_ids = in_rows(got_meta[:, 0, :])
    got_w = in_rows(got_meta[:, 1, :])
    active = (jnp.max(got_w, axis=2) > 0).astype(I32).reshape(-1)

    prods, new_table, new_states = pl.pallas_call(
        owner_kernel,
        grid_spec=pltpu.PrefetchScalarGridSpec(
            num_scalar_prefetch=2,
            grid=(groups,),
            in_specs=[
                pl.BlockSpec((1, 8, k2), lambda c, *_: (c, 0, 0)),
                pl.BlockSpec((1, 8, k2), lambda c, *_: (c, 0, 0)),
                pl.BlockSpec((srcs, width, n_bags), lambda c, *_: (c, 0, 0)),
                pl.BlockSpec((touched, width), lambda c, *_: (0, 0)),
                pl.BlockSpec((touched // 128, 128), lambda c, *_: (0, 0)),
            ],
            out_specs=(
                pl.BlockSpec((1, 8, k2), lambda c, *_: (c, 0, 0)),
                pl.BlockSpec((touched, width), lambda c, *_: (0, 0)),
                pl.BlockSpec((touched // 128, 128), lambda c, *_: (0, 0)),
            ),
            scratch_shapes=[
                pltpu.VMEM((2 * width, touched), BF),
                pltpu.VMEM((width, touched), F32),
                pltpu.VMEM((touched, 2 * k2), BF),
            ],
        ),
        out_shape=(
            jax.ShapeDtypeStruct((groups, 8, k2), F32),
            jax.ShapeDtypeStruct((touched, width), F32),
            jax.ShapeDtypeStruct((touched // 128, 128), F32),
        ),
        compiler_params=params("arbitrary"),
        name="owner_step",
    )(active, counts, got_ids, got_w, everyone, table, states.reshape(touched // 128, 128))

    back = jnp.concatenate(
        [
            prods[:, 0:4].reshape(devices, 64),
            prods[:, 4].reshape(devices, 16),
            prods[:, 5].reshape(devices, 16),
        ],
        axis=1,
    )
    back = jnp.pad(back, ((0, 0), (0, RP - CAP)))
    returned = lax.all_to_all(back, BOTH, split_axis=0, concat_axis=0, tiled=True)
    weight_grad = pl.pallas_call(
        back_kernel,
        out_shape=jax.ShapeDtypeStruct((steps, k1), F32),
        in_specs=[vmem] * 4,
        out_specs=vmem,
        scratch_shapes=[pltpu.VMEM((2 * RP, devices), BF)],
        name="back",
    )(key, rank, w, returned)
    return (weight_grad.reshape(weights.shape), new_table, new_states.reshape(-1))


def solution(mesh):
    return jax.shard_map(
        local,
        mesh=mesh,
        in_specs=(
            P(BOTH, None, None),
            P(BOTH, None, None),
            P(BOTH, None, None),
            P(BOTH, None, None),
            P(BOTH, None),
            P(BOTH),
            P(BOTH, None),
            P(BOTH),
        ),
        out_specs=(P(BOTH, None, None), P(BOTH, None), P(BOTH)),
        check_vma=False,
    )
```
